32 devices in a mesh: dp: 16 (over z, y, core), mp: 2 (over x).
Axes of the slice: x: 2, y: 2, z: 4, core: 2. Of those that a mesh axis runs over, the one named last changes fastest.
Arguments:
- hidden_in: bfloat16 [8192, 4096], P('dp'), may hold values from -1.5 to 1.5
- w_query: bfloat16 [4096, 4096], P('dp', 'mp'), may hold values from -1 to 1
- w_key: bfloat16 [4096, 1024], P('dp', 'mp'), may hold values from -24 to 24
- w_value: bfloat16 [4096, 1024], P('dp', 'mp'), may hold values from -1 to 1
- w_out: bfloat16 [4096, 4096], P('dp', 'mp'), may hold values from -1 to 1
- value_weight: float32 [4096], P('mp'), may hold values from -0.09375 to 0.09375
- rewards: float32 [8192], P('dp'), may hold values from -0.6 to 0.6
- old_values: float32 [8192], P('dp'), may hold values from -6 to 6
- lengths: int32 [64], replicated, may hold values from 1 to 2048, 8192 in all
- terminal: int32 [64], replicated, may hold values 0 or 1
Outputs:
- value: float32 [8192], P('dp')
- advantage: float32 [8192], P('dp')
- value_loss: float32 [], replicated
The draws below stay inside these ranges and needn't reach their ends.
All inputs are finite; a program needn't handle non-finite values.
Results may differ from the reference program's by a relative error of at most 0.012.
The reference program's roundings to bfloat16 on the way (of `normed`, `values_proj`, `probs` and `attended`) count: a program that leaves them out, or rounds other values in their place, can miss the bound.
Values may be sent and summed in bfloat16 or wider, within the bound.
No kernel may reach another device: no remote copies, remote signals or barrier semaphores. Data moves between devices by JAX's collectives and lax.ppermute only.
A program may use at most 128 MiB of HBM per device.

```python
import math
import jax
import jax.numpy as jnp
import numpy as np
from jax import lax

D = 4096
HEADS = 32
KV_HEADS = 8
HEAD = 128
TOK_DEV = 512
MAX_LEN = 2048
EPISODES = 64
TOKENS = 8192
N_DP = 16


def shared_query(key):
    base = jax.random.fold_in(key, 11)
    sample = jnp.clip(jax.random.normal(base, (D, HEADS * HEAD), jnp.float32), -4.0, 4.0)
    return sample * D ** (-0.5)


def mixed_blocks(key, common_shape, full_shape):
    common_key = jax.random.fold_in(key, 1)
    private_key = jax.random.fold_in(key, 2)
    common = jnp.clip(jax.random.normal(common_key, common_shape, jnp.float32), -4.0, 4.0)
    private = jnp.clip(jax.random.normal(private_key, full_shape, jnp.float32), -4.0, 4.0)
    return 0.8 * common + 0.6 * private


def draw_w_query(key, part):
    return shared_query(key).astype(jnp.bfloat16)


def draw_w_key(key, part):
    noise = jnp.clip(jax.random.normal(jax.random.fold_in(key, 23), (D, KV_HEADS * HEAD), jnp.float32), -4.0, 4.0) * D ** (-0.5)
    return noise.astype(jnp.bfloat16)


def draw_w_value(key, part):
    sample = mixed_blocks(jax.random.fold_in(key, 51), (D, 1, HEAD), (D, KV_HEADS, HEAD))
    return (sample.reshape(D, KV_HEADS * HEAD) * D ** (-0.5)).astype(jnp.bfloat16)


def draw_w_out(key, part):
    sample = mixed_blocks(jax.random.fold_in(key, 67), (1, HEAD, D), (HEADS, HEAD, D))
    return (sample.reshape(HEADS * HEAD, D) * (HEADS * HEAD) ** (-0.5)).astype(jnp.bfloat16)


def touch_ends(result, own_key, least, high):
    extent = result.shape
    spot = [jax.random.randint(jax.random.fold_in(own_key, axis), (), 0, extent[axis]) for axis in range(len(extent))]
    result = result.at[tuple(spot)].set(least)
    longest = extent.index(max(extent))
    spot[longest] = (spot[longest] + 1) % extent[longest]
    return result.at[tuple(spot)].set(high)


def block_scale(rng, extent, shards, low, high):
    def one(dim, parts):
        steps = jax.random.uniform(jax.random.fold_in(jax.random.fold_in(rng, 6), dim), (parts,), jnp.float32, low / len(shards), high / len(shards))
        return jnp.repeat(jnp.exp(steps), extent[dim] // parts).reshape((-1,) + (1,) * (len(extent) - dim - 1))

    level = one(*shards[0])
    for cut in shards[1:]:
        level = level * one(*cut)
    return level


def profile(amount, total, limit, lean):
    portions = [(1 << 20) // math.isqrt(rank ** lean) + 1 for rank in range(2, amount + 1)]
    rest, given = total - limit - (amount - 1), [1] * (amount - 1)
    while rest > 0:
        candidates = [i for i in range(amount - 1) if given[i] < limit]
        pool, left = sum([portions[i] for i in candidates]), rest
        for i in candidates:
            extra = min(limit - given[i], max(1, left * portions[i] // pool), rest)
            given[i] = given[i] + extra
            rest = rest - extra
    return np.array([limit] + given)


def ragged_sizes(rng, number_of, total, reach, lean):
    if number_of == 2:
        one = jax.random.randint(rng, (), max(1, total - reach), min(reach, total - 1) + 1)
        return jnp.stack([one, total - one])
    tallies = jnp.asarray(profile(number_of, total, reach, lean), jnp.int32)
    couples = (number_of - 1) // 2
    giver, sink = tallies[1:1 + 2 * couples:2], tallies[2:2 + 2 * couples:2]
    slack = jnp.minimum(giver - 1, reach - sink)
    moved = jax.random.randint(jax.random.fold_in(rng, 1), (couples,), 0, 1 << 20) % (slack + 1)
    tallies = tallies.at[1:1 + 2 * couples:2].set(giver - moved).at[2:2 + 2 * couples:2].set(sink + moved)
    return tallies[jax.random.permutation(jax.random.fold_in(rng, 2), number_of)]


def bell_draw(rng, extent, scale, reach, cuts=(), held_as=jnp.bfloat16):
    result = scale * jax.random.normal(rng, extent, jnp.float32)
    if cuts:
        result = result * block_scale(rng, extent, cuts, -0.22, 0.18)
    return jnp.clip(result, -reach, reach).astype(held_as)


def setup_inputs(seed: int = 0) -> dict:
    streams_of = jax.random.split(jax.random.key(seed), 11)
    return {
        "hidden_in": bell_draw(streams_of[0], (TOKENS, D), 0.25, 1.5, ((0, 16),)),
        "w_query": draw_w_query(jax.random.fold_in(streams_of[10], 71), 0),
        "w_key": draw_w_key(jax.random.fold_in(streams_of[10], 71), 0),
        "w_value": draw_w_value(jax.random.fold_in(streams_of[10], 71), 0),
        "w_out": draw_w_out(jax.random.fold_in(streams_of[10], 71), 0),
        "value_weight": bell_draw(streams_of[5], (D,), D ** -0.5, 0.09375, ((0, 2),), jnp.float32),
        "rewards": bell_draw(streams_of[6], (TOKENS,), 0.1, 0.6, ((0, 16),), jnp.float32),
        "old_values": bell_draw(streams_of[7], (TOKENS,), 1.0, 6.0, ((0, 16),), jnp.float32),
        "lengths": ragged_sizes(streams_of[8], EPISODES, TOKENS, MAX_LEN, 2).astype(jnp.int32),
        "terminal": touch_ends((jax.random.randint(streams_of[9], (EPISODES,), 0, 2) < 1).astype(jnp.int32), jax.random.fold_in(streams_of[9], 1), 0, 1),
    }


discount = 0.999
trace_decay = 0.997
clip_range = 0.2
epsilon = 1e-05
rope_base = 500000.0

def rotate(states, positions):
    half = HEAD // 2
    freq = rope_base ** (-jnp.arange(half, dtype=jnp.float32) * 2.0 / HEAD)
    angles = positions[:, None] * freq[None, :]
    cosine = jnp.cos(angles)[:, None, :]
    sine = jnp.sin(angles)[:, None, :]
    first = states[..., :half]
    second = states[..., half:]
    return jnp.concatenate([first * cosine - second * sine, second * cosine + first * sine], -1)

def episode_marks(lengths, terminal, position_ids):
    ends = jnp.cumsum(lengths).astype(jnp.int32)
    matches = ends[None, :] - 1 == position_ids[:, None]
    finished = jnp.any(matches, 1).astype(jnp.float32)
    stopped = lax.optimization_barrier(jnp.sum(jnp.where(matches, terminal[None, :], 0), 1)).astype(jnp.float32)
    episode = lax.optimization_barrier(jnp.sum((ends[None, :] <= position_ids[:, None]).astype(jnp.int32), 1))
    return (finished, stopped, episode)

def attend_window(inputs):
    query, key, values_proj, episode = inputs
    rows = query.shape[0]
    group = HEADS // KV_HEADS
    q_four = query.astype(jnp.float32).reshape(rows, KV_HEADS, group, HEAD)
    k_four = key.astype(jnp.float32).reshape(rows, KV_HEADS, HEAD)
    v_four = values_proj.astype(jnp.float32).reshape(rows, KV_HEADS, HEAD)
    scores = jnp.einsum('tkgd,skd->kgts', q_four, k_four) * (1.0 / HEAD ** 0.5)
    order = jnp.arange(rows, dtype=jnp.int32)
    allowed = (order[None, :] <= order[:, None]) & (episode[None, :] == episode[:, None])
    masked = jnp.where(allowed[None, None], scores, -1e+30)
    largest = lax.optimization_barrier(jnp.max(masked, -1, keepdims=True))
    expon = jnp.where(allowed[None, None], jnp.exp(masked - largest), 0.0)
    probs = (expon / lax.optimization_barrier(jnp.sum(expon, -1, keepdims=True))).astype(jnp.bfloat16)
    output = jnp.einsum('kgts,skd->tkgd', probs.astype(jnp.float32), v_four)
    return output.astype(jnp.bfloat16).reshape(rows, HEADS * HEAD)

def reference(hidden_in, w_query, w_key, w_value, w_out, value_weight, rewards, old_values, lengths, terminal):
    states = hidden_in.astype(jnp.float32)
    normed = (states * lax.rsqrt(lax.optimization_barrier(jnp.mean(states * states, 1, keepdims=True)) + epsilon)).astype(jnp.bfloat16)
    position_ids = jnp.arange(TOKENS, dtype=jnp.int32)
    positions = position_ids.astype(jnp.float32)
    query = jnp.dot(normed, w_query, preferred_element_type=jnp.float32).reshape(TOKENS, HEADS, HEAD)
    query = rotate(query, positions).astype(jnp.bfloat16)
    key = jnp.dot(normed, w_key, preferred_element_type=jnp.float32).reshape(TOKENS, KV_HEADS, HEAD)
    key = rotate(key, positions).astype(jnp.bfloat16)
    values_proj = jnp.dot(normed, w_value, preferred_element_type=jnp.float32).astype(jnp.bfloat16)
    finished, stopped, episode = episode_marks(lengths, terminal, position_ids)
    windows = (query.reshape(N_DP, TOK_DEV, HEADS * HEAD), key.reshape(N_DP, TOK_DEV, KV_HEADS * HEAD), values_proj.reshape(N_DP, TOK_DEV, KV_HEADS * HEAD), episode.reshape(N_DP, TOK_DEV))
    attended = lax.map(attend_window, windows).reshape(TOKENS, HEADS * HEAD)
    residual = states + jnp.dot(attended, w_out, preferred_element_type=jnp.float32)
    value = lax.optimization_barrier(jnp.sum(residual * value_weight[None, :], 1)) * lax.rsqrt(lax.optimization_barrier(jnp.mean(residual * residual, 1)) + epsilon)
    next_old = jnp.concatenate([old_values[1:], jnp.zeros((1,), jnp.float32)])
    booted = jnp.where(finished > 0, (1.0 - stopped) * old_values, next_old)
    delta = rewards + discount * booted - old_values
    carried = discount * trace_decay * (1.0 - finished)

    def backward(carry, item):
        step_delta, step_keep = item
        fresh = step_delta + step_keep * carry
        return (fresh, fresh)
    _, advantage = lax.scan(backward, jnp.zeros((), jnp.float32), (delta, carried), reverse=True)
    returns = advantage + old_values
    clipped = old_values + jnp.clip(value - old_values, -clip_range, clip_range)
    terms = jnp.maximum((value - returns) ** 2, (clipped - returns) ** 2)
    value_loss = 0.5 * jnp.sum(terms) / TOKENS
    return (value, advantage, value_loss)
```

```python
import jax
import jax.numpy as jnp
from jax import lax
from jax.experimental import pallas as pl
from jax.experimental.pallas import tpu as pltpu
from jax.sharding import PartitionSpec as P

HEAD = 128


discount = 0.999
trace_decay = 0.997
clip_range = 0.2
epsilon = 1e-05
rope_base = 500000.0


def from_behind(array, axis, by):
    size = lax.axis_size(axis)
    pairs = [(i, i + by) for i in range(size) if 0 <= i + by < size]
    return lax.ppermute(array, axis, pairs)


def carried_in(part, axis, combine, identity):
    count = lax.axis_size(axis)
    place = lax.axis_index(axis)
    ahead = count - 1 - place
    gathered = jax.tree.map(lambda a: lax.all_gather(a, axis), part)
    state = jax.tree.map(lambda a, e: jnp.zeros_like(a) + jnp.asarray(e, a.dtype), part, identity)

    def one(hop, state):
        source = count - 1 - hop
        return combine(
            state, jax.tree.map(lambda a: lax.dynamic_index_in_dim(a, source, 0, False), gathered)
        )

    return lax.fori_loop(0, ahead, one, state)


def rotate(states, positions):
    half = HEAD // 2
    freq = rope_base ** (-jnp.arange(half, dtype=jnp.float32) * 2.0 / HEAD)
    angles = positions[:, None] * freq[None, :]
    cosine = jnp.cos(angles)[:, None, :]
    sine = jnp.sin(angles)[:, None, :]
    first = states[..., :half]
    second = states[..., half:]
    return jnp.concatenate([first * cosine - second * sine, second * cosine + first * sine], -1)


def plain_body(
    hidden_in, w_query, w_key, w_value, w_out, value_weight, rewards, old_values, lengths, terminal
):
    rows = hidden_in.shape[0]
    width = hidden_in.shape[1]
    states = hidden_in.astype(jnp.float32)
    normed = (states * lax.rsqrt(jnp.mean(states * states, 1, keepdims=True) + epsilon)).astype(
        jnp.bfloat16
    )
    pieces = (
        lax.all_gather(w_query, "dp", axis=0, tiled=True),
        lax.all_gather(w_key, "dp", axis=0, tiled=True),
        lax.all_gather(w_value, "dp", axis=0, tiled=True),
        lax.all_gather(w_out, "dp", axis=0, tiled=True),
    )
    add_pieces = pieces[:3]
    summed = tuple(
        (jnp.dot(normed, piece, preferred_element_type=jnp.float32) for piece in add_pieces)
    )
    stored = pieces[3]
    query_sum, key_sum, value_sum, whole_out = summed + (stored,)
    position_ids = lax.axis_index("dp") * rows + jnp.arange(rows, dtype=jnp.int32)
    positions = position_ids.astype(jnp.float32)
    local_heads = w_query.shape[1] // HEAD
    local_kv = w_key.shape[1] // HEAD
    group = local_heads // local_kv
    query = rotate(query_sum.reshape(rows, local_heads, HEAD), positions).astype(jnp.bfloat16)
    key = rotate(key_sum.reshape(rows, local_kv, HEAD), positions).astype(jnp.bfloat16)
    values_proj = value_sum.astype(jnp.bfloat16).reshape(rows, local_kv, HEAD)
    ends = jnp.cumsum(lengths)
    matches = ends[None, :] - 1 == position_ids[:, None]
    finished = jnp.any(matches, 1).astype(jnp.float32)
    stopped = jnp.sum(jnp.where(matches, terminal[None, :], 0), 1).astype(jnp.float32)
    episode = jnp.sum((ends[None, :] <= position_ids[:, None]).astype(jnp.int32), 1)
    order = jnp.arange(rows, dtype=jnp.int32)
    same_episode = episode[None, :] == episode[:, None]
    allowed = (order[None, :] <= order[:, None]) & same_episode
    scores = jnp.einsum(
        "tkgd,skd->kgts",
        query.reshape(rows, local_kv, group, HEAD),
        key,
        preferred_element_type=jnp.float32,
    ) * (1.0 / HEAD**0.5)
    masked = jnp.where(allowed[None, None], scores, -1e30)
    largest = jnp.max(masked, -1, keepdims=True)
    expon = jnp.where(allowed[None, None], jnp.exp(masked - largest), 0.0)
    probs = (expon / jnp.sum(expon, -1, keepdims=True)).astype(jnp.bfloat16)
    output = jnp.einsum("kgts,skd->tkgd", probs, values_proj, preferred_element_type=jnp.float32)
    attended = output.astype(jnp.bfloat16).reshape(rows, local_heads * HEAD)
    all_heads = lax.all_gather(attended, "mp", axis=1, tiled=True)
    projected = jnp.dot(all_heads, whole_out, preferred_element_type=jnp.float32)
    feature_count = w_out.shape[1]
    own_states = lax.dynamic_slice_in_dim(
        states, lax.axis_index("mp") * feature_count, feature_count, 1
    )
    residual = own_states + projected
    square_sum, head_sum = lax.psum(
        (jnp.sum(residual * residual, 1), jnp.sum(residual * value_weight[None, :], 1)), "mp"
    )
    value = head_sum * lax.rsqrt(square_sum / width + epsilon)
    following = from_behind(old_values[:1], "dp", -1)
    next_old = jnp.concatenate([old_values[1:], following])
    booted = jnp.where(finished > 0, (1.0 - stopped) * old_values, next_old)
    delta = rewards + discount * booted - old_values
    keep_rate = discount * trace_decay
    spacing = (order[None, :] - order[:, None]).astype(jnp.float32)
    forward_mask = (spacing >= 0.0) & same_episode
    decay_matrix = jnp.where(
        forward_mask, jnp.power(jnp.float32(keep_rate), jnp.maximum(spacing, 0.0)), 0.0
    )
    local_part = jnp.dot(decay_matrix, delta, precision=lax.Precision.HIGHEST)
    remaining = (rows - order).astype(jnp.float32)
    reach = jnp.where(episode == episode[-1], jnp.power(jnp.float32(keep_rate), remaining), 0.0) * (
        1.0 - finished[-1]
    )

    def compose(earlier, later_map):
        return (later_map[0] + later_map[1] * earlier[0], later_map[1] * earlier[1])

    prefix = carried_in(
        (local_part[:1], reach[:1]),
        "dp",
        compose,
        (jnp.zeros((1,), jnp.float32), jnp.ones((1,), jnp.float32)),
    )
    incoming = prefix[0][0]
    advantage = local_part + reach * incoming
    returns = advantage + old_values
    clipped = old_values + jnp.clip(value - old_values, -clip_range, clip_range)
    terms = jnp.maximum((value - returns) ** 2, (clipped - returns) ** 2)
    total_loss = lax.psum(jnp.sum(terms), "dp")
    value_loss = 0.5 * total_loss / (rows * lax.axis_size("dp"))
    return (value, advantage, value_loss)


def ring_order(chips):
    return list(range(0, chips, 2)) + list(range(chips - 1, 0, -2))


def ring_pairs(chips):
    order = ring_order(chips)
    pairs = []
    for spot in range(chips):
        here, there = order[spot], order[(spot + 1) % chips]
        pairs.append((2 * here, 2 * there))
        pairs.append((2 * there + 1, 2 * here + 1))
    return pairs


def ring_sources(chips):
    order = ring_order(chips)
    spots = {chip: spot for spot, chip in enumerate(order)}
    forward = [[order[(spots[c] - k) % chips] for k in range(chips)] for c in range(chips)]
    back = [[order[(spots[c] + k) % chips] for k in range(chips)] for c in range(chips)]
    return jnp.array([forward, back], jnp.int32)


def norm_kernel(sources, states_ref, normed_ref):
    width = states_ref.shape[1]
    chips = sources.shape[0]
    span = width // chips
    states = states_ref[...].astype(jnp.float32)
    scale = lax.rsqrt(jnp.mean(states * states, 1, keepdims=True) + epsilon)
    for k in range(chips):
        start = pl.multiple_of(sources[k] * span, span)
        piece = states_ref[:, pl.ds(start, span)].astype(jnp.float32)
        normed_ref[:, k * span : (k + 1) * span] = (piece * scale).astype(jnp.bfloat16)


def norm_in_order(states, sources):
    rows, width = states.shape
    tile = min(128, rows)
    return pl.pallas_call(
        norm_kernel,
        grid_spec=pltpu.PrefetchScalarGridSpec(
            num_scalar_prefetch=1,
            grid=(rows // tile,),
            in_specs=[pl.BlockSpec((tile, width), lambda i, s: (i, 0))],
            out_specs=pl.BlockSpec((tile, width), lambda i, s: (i, 0)),
        ),
        out_shape=jax.ShapeDtypeStruct((rows, width), jnp.bfloat16),
        cost_estimate=pl.CostEstimate(
            flops=4 * rows * width, bytes_accessed=4 * rows * width, transcendentals=rows
        ),
        name="norm",
    )(sources, states)


def spin(states, cosine, sine):
    return states * cosine + pltpu.roll(states, HEAD // 2, 1) * sine


def attend_kernel(group, kv_count, *refs):
    query_refs = refs[:kv_count]
    kv_ref, cos_ref, sin_ref, ep_col_ref, ep_row_ref, out_ref, bias_ref = refs[kv_count:]
    rows = kv_ref.shape[0]
    tile = rows // 2
    cosine = cos_ref[...]
    sine = sin_ref[...]
    at_row = lax.broadcasted_iota(jnp.int32, (rows, rows), 0)
    at_col = lax.broadcasted_iota(jnp.int32, (rows, rows), 1)
    allowed = (at_col <= at_row) & (ep_col_ref[...] == ep_row_ref[...])
    bias_ref[...] = jnp.where(allowed, 0.0, -1e30)
    for j in range(kv_count):
        key = spin(kv_ref[:, j * HEAD : (j + 1) * HEAD], cosine, sine).astype(jnp.bfloat16)
        first = (kv_count + j) * HEAD
        vals = kv_ref[:, first : first + HEAD].astype(jnp.bfloat16)
        for h in range(group):
            query = spin(
                query_refs[j][:, h * HEAD : (h + 1) * HEAD], cosine, sine
            ).astype(jnp.bfloat16)
            column = (j * group + h) * HEAD
            for t in range(2):
                low, high = t * tile, (t + 1) * tile
                scores = lax.dot_general(
                    query[low:high],
                    key[:high],
                    (((1,), (1,)), ((), ())),
                    preferred_element_type=jnp.float32,
                )
                masked = scores * (1.0 / HEAD**0.5) + bias_ref[low:high, :high]
                largest = jnp.max(masked, -1, keepdims=True)
                expon = jnp.exp(masked - largest)
                share = 1.0 / jnp.sum(expon, -1, keepdims=True)
                probs = (expon * share).astype(jnp.bfloat16)
                out_ref[low:high, column : column + HEAD] = jnp.dot(
                    probs, vals[:high], preferred_element_type=jnp.float32
                ).astype(jnp.bfloat16)


def attend(window, rows, group, queries, kv, cosine, sine, ep_col, ep_row):
    kv_count = len(queries)
    heads = group * kv_count
    once = lambda i: (window, 0)
    return pl.pallas_call(
        lambda *refs: attend_kernel(group, kv_count, *refs),
        grid=(1,),
        in_specs=[pl.BlockSpec((rows, q.shape[1]), once) for q in queries]
        + [
            pl.BlockSpec((rows, kv.shape[1]), once),
            pl.BlockSpec((rows, HEAD), once),
            pl.BlockSpec((rows, HEAD), once),
            pl.BlockSpec((rows, 1), once),
            pl.BlockSpec((1, rows), lambda i: (0, window)),
        ],
        out_specs=pl.BlockSpec((rows, heads * HEAD), lambda i: (0, 0)),
        out_shape=jax.ShapeDtypeStruct((rows, heads * HEAD), jnp.bfloat16),
        scratch_shapes=[pltpu.VMEM((rows, rows), jnp.float32)],
        cost_estimate=pl.CostEstimate(
            flops=4 * heads * HEAD * rows * rows,
            bytes_accessed=4 * rows * HEAD * heads * 2,
            transcendentals=heads * rows * rows,
        ),
        name=f"attend{window}",
    )(*queries, kv, cosine, sine, ep_col, ep_row)


def project_kernel(count, has_base, last, *refs):
    offsets = refs[0]
    heads_ref = refs[1]
    pairs = refs[2 : 2 + 2 * count]
    rest = refs[2 + 2 * count :]
    span, half = pairs[0].shape
    for side in range(2):
        total = rest[0][:, side * half : (side + 1) * half] if has_base else 0.0
        for k in range(count):
            start = pl.multiple_of(offsets[k], span)
            total = total + jnp.dot(
                heads_ref[:, pl.ds(start, span)],
                pairs[2 * k + side][...],
                preferred_element_type=jnp.float32,
            )
        if not last:
            rest[-1][:, side * half : (side + 1) * half] = total
            continue
        states_ref, weight_ref, out_ref = rest[1:]
        residual = total + states_ref[:, side * half : (side + 1) * half].astype(jnp.float32)
        weight = weight_ref[:, side * half : (side + 1) * half]
        squares = jnp.sum(residual * residual, 1, keepdims=True)
        headed = jnp.sum(residual * weight, 1, keepdims=True)
        if side == 0:
            out_ref[:, 0:1] = squares
            out_ref[:, 1:2] = headed
        else:
            out_ref[:, 0:1] += squares
            out_ref[:, 1:2] += headed


def project(offsets, heads, pairs, base=None, final=None):
    tokens, width = heads.shape
    count = len(pairs)
    tile = min(256, tokens)
    columns = 2 * pairs[0][0].shape[1]
    by_tile = lambda i, s: (i, 0)
    whole = lambda i, s: (0, 0)
    operands = [heads] + [w for pair in pairs for w in pair]
    specs = [pl.BlockSpec((tile, width), by_tile)]
    specs += [pl.BlockSpec(w.shape, whole) for w in operands[1:]]
    if base is not None:
        operands.append(base)
        specs.append(pl.BlockSpec((tile, columns), by_tile))
    if final is None:
        out_spec = pl.BlockSpec((tile, columns), by_tile)
        out_shape = jax.ShapeDtypeStruct((tokens, columns), jnp.float32)
    else:
        operands += list(final)
        specs += [pl.BlockSpec((tile, columns), by_tile), pl.BlockSpec((1, columns), whole)]
        out_spec = pl.BlockSpec((tile, 2), by_tile)
        out_shape = jax.ShapeDtypeStruct((tokens, 2), jnp.float32)
    span = pairs[0][0].shape[0]
    return pl.pallas_call(
        lambda *refs: project_kernel(count, base is not None, final is not None, *refs),
        grid_spec=pltpu.PrefetchScalarGridSpec(
            num_scalar_prefetch=1, grid=(tokens // tile,), in_specs=specs, out_specs=out_spec
        ),
        out_shape=out_shape,
        cost_estimate=pl.CostEstimate(
            flops=2 * tokens * columns * span * count,
            bytes_accessed=2 * tokens * span * count + 4 * tokens * columns,
            transcendentals=0,
        ),
        name="project_last" if final is not None else "project",
    )(offsets, *operands)


def shared_body(
    hidden_in, w_query, w_key, w_value, w_out, value_weight, rewards, old_values, lengths, terminal
):
    rows, width = hidden_in.shape
    devices = lax.axis_size("dp")
    place = lax.axis_index("dp")
    side = lax.axis_index("mp")
    core = place % 2
    chip = place // 2
    chips = devices // 2
    partner = [(i, i ^ 1) for i in range(devices)]
    across = [(0, 1), (1, 0)]
    ring = ring_pairs(chips)
    sources = ring_sources(chips)[core, chip]

    def swap(array):
        return lax.ppermute(array, "dp", partner)

    def pair_up(mine, got):
        return jnp.where(
            core == 0, jnp.concatenate([mine, got], 0), jnp.concatenate([got, mine], 0)
        )

    def columns(weight, which, part, parts):
        half = weight.shape[1] // 2
        size = half // parts
        return lax.dynamic_slice_in_dim(weight, which * half + part * size, size, 1)

    def chip_block(pieces):
        mine = jnp.concatenate([columns(w, core, *p) for w, *p in pieces], 1)
        theirs = jnp.concatenate([columns(w, 1 - core, *p) for w, *p in pieces], 1)
        return pair_up(mine, swap(theirs))

    local_kv = w_key.shape[1] // HEAD // 2
    group = w_query.shape[1] // w_key.shape[1]
    lanes = [chip_block([(w_key, 0, 1), (w_value, 0, 1)])]
    lanes += [chip_block([(w_query, j, local_kv)]) for j in range(local_kv)]
    out_lanes = [chip_block([(w_out, j, 2)]) for j in range(2)]

    def travel(block, after=None):
        blocks = [block]
        for hop in range(1, chips):
            blocks.append(lax.ppermute(blocks[-1], "dp", ring))
        return blocks

    first = [travel(block) for block in lanes]
    held = lax.optimization_barrier(tuple(out_lanes) + (first[-1][chips - 2],))
    last = [travel(block) for block in held[:2]]

    normed_own = norm_in_order(hidden_in, sources)
    normed_got = swap(normed_own)
    span = width // chips
    sums = []
    for blocks in first:
        total = None
        for k, block in enumerate(blocks):
            back = (chips - k) % chips
            both = jnp.concatenate(
                [
                    normed_own[:, k * span : (k + 1) * span],
                    normed_got[:, back * span : (back + 1) * span],
                ],
                0,
            )
            term = jnp.dot(both, block, preferred_element_type=jnp.float32)
            total = term if total is None else total + term
        sums.append(total)

    ends = jnp.cumsum(lengths)
    order = jnp.arange(rows, dtype=jnp.int32)
    position_ids = place * rows + order
    other_ids = (place + 1 - 2 * core) * rows + order
    both_ids = jnp.concatenate([position_ids, other_ids])
    half = HEAD // 2
    freq = rope_base ** (-jnp.arange(half, dtype=jnp.float32) * 2.0 / HEAD)
    angles = both_ids.astype(jnp.float32)[:, None] * freq[None, :]
    cosine = jnp.cos(angles)
    sine = jnp.sin(angles)
    cosine = jnp.concatenate([cosine, cosine], 1)
    sine = jnp.concatenate([-sine, sine], 1)
    both_episode = jnp.sum((ends[None, :] <= both_ids[:, None]).astype(jnp.int32), 1)

    mine = [
        attend(
            w, rows, group, sums[1:], sums[0], cosine, sine,
            both_episode[:, None], both_episode[None, :],
        )
        for w in range(2)
    ]
    beside = [swap(mine[1]), swap(mine[0])]
    opposite = [lax.ppermute(m, "mp", across) for m in mine]
    diagonal = [swap(opposite[1]), swap(opposite[0])]
    all_heads = jnp.concatenate(
        [jnp.concatenate(list(p), 1) for p in zip(mine, beside, opposite, diagonal)], 0
    )
    quarter = mine[0].shape[1]
    own_quarter = side * 2 + core
    offsets = ((sources * span // quarter) ^ own_quarter) * quarter + sources * span % quarter
    out_pairs = list(zip(*last))
    early = chips - 2
    part = project(offsets[:early], all_heads, out_pairs[:early])

    out_columns = w_out.shape[1] // 2
    states_own = lax.dynamic_slice_in_dim(hidden_in, own_quarter * out_columns, out_columns, 1)
    states_sent = lax.dynamic_slice_in_dim(
        hidden_in, (own_quarter ^ 1) * out_columns, out_columns, 1
    )
    states_both = jnp.concatenate([states_own, swap(states_sent)], 0)
    weight_own = lax.dynamic_slice_in_dim(value_weight, core * out_columns, out_columns, 0)
    pair_sums = project(
        offsets[early:], all_heads, out_pairs[early:], part, (states_both, weight_own[None, :])
    ).T

    matches = ends[None, :] - 1 == position_ids[:, None]
    finished = jnp.any(matches, 1).astype(jnp.float32)
    stopped = jnp.sum(jnp.where(matches, terminal[None, :], 0), 1).astype(jnp.float32)
    episode = both_episode[:rows]
    same_episode = episode[None, :] == episode[:, None]
    next_known = jnp.concatenate([old_values[1:], jnp.zeros((1,), jnp.float32)])
    booted = jnp.where(finished > 0, (1.0 - stopped) * old_values, next_known)
    delta = rewards + discount * booted - old_values
    keep_rate = discount * trace_decay
    spacing = (order[None, :] - order[:, None]).astype(jnp.float32)
    forward_mask = (spacing >= 0.0) & same_episode
    decay_matrix = jnp.where(
        forward_mask, jnp.power(jnp.float32(keep_rate), jnp.maximum(spacing, 0.0)), 0.0
    )
    local_part = jnp.dot(decay_matrix, delta, precision=lax.Precision.HIGHEST)
    remaining = (rows - order).astype(jnp.float32)
    open_end = 1.0 - finished[-1]
    reach = jnp.where(episode == episode[-1], jnp.power(jnp.float32(keep_rate), remaining), 0.0) * open_end
    bridge = reach / trace_decay
    state = jnp.stack([local_part[0], bridge[0], reach[0], old_values[0]])
    identity = jnp.array([0.0, 0.0, 1.0, 0.0], jnp.float32)

    def from_after(array, by):
        moved = lax.ppermute(array, "dp", [((i + by) % devices, i) for i in range(devices)])
        return jnp.where(place + by < devices, moved, identity)

    state = from_after(state, 1)
    by = 1
    while by < devices:
        far = from_after(state, by)
        joined = jnp.stack(
            [
                state[0] + state[1] * far[3] + state[2] * far[0],
                state[2] * far[1],
                state[2] * far[2],
                state[3],
            ]
        )
        state = jnp.where(place + by < devices - 1, joined, state)
        by *= 2
    advantage = local_part + bridge * state[3] + reach * state[0]

    shared = swap(jnp.stack([advantage, old_values]))
    both_advantage = jnp.stack([advantage, shared[0]])
    both_old = jnp.stack([old_values, shared[1]])

    pair_sums = pair_sums + lax.ppermute(pair_sums, "mp", across)
    turned = swap(pair_sums)
    pair_sums = pair_sums.reshape(2, 2, rows) + turned.reshape(2, 2, rows)[:, ::-1]
    value = pair_sums[1] * lax.rsqrt(pair_sums[0] / width + epsilon)
    returns = both_advantage + both_old
    clipped = both_old + jnp.clip(value - both_old, -clip_range, clip_range)
    terms = jnp.maximum((value - returns) ** 2, (clipped - returns) ** 2)
    window_loss = jnp.sum(terms, 1)
    total_loss = window_loss[:1] + window_loss[1:]
    by = 2
    while by < devices:
        total_loss = total_loss + lax.ppermute(
            total_loss, "dp", [(i, i ^ by) for i in range(devices)]
        )
        by *= 2
    value_loss = 0.5 * total_loss[0] / (rows * devices)
    return (value[0], advantage, value_loss)


def body(hidden_in, w_query, w_key, *rest):
    devices = lax.axis_size("dp")
    fits = (
        lax.axis_size("mp") == 2
        and devices >= 4
        and devices & (devices - 1) == 0
        and w_key.shape[1] % (2 * HEAD) == 0
        and hidden_in.shape[0] % 256 == 0
        and 2 * hidden_in.shape[1] % devices == 0
    )
    return (shared_body if fits else plain_body)(hidden_in, w_query, w_key, *rest)


def solution(mesh):
    return jax.shard_map(
        body,
        mesh=mesh,
        in_specs=(
            P("dp", None),
            P("dp", "mp"),
            P("dp", "mp"),
            P("dp", "mp"),
            P("dp", "mp"),
            P("mp"),
            P("dp"),
            P("dp"),
            P(),
            P(),
        ),
        out_specs=(P("dp"), P("dp"), P()),
        check_vma=False,
    )
```

```python
import jax
import jax.numpy as jnp
from jax import lax
from jax.experimental import pallas as pl
from jax.experimental.pallas import tpu as pltpu
from jax.sharding import PartitionSpec as P


HEAD = 128


discount = 0.999
trace_decay = 0.997
clip_range = 0.2
epsilon = 1e-05
rope_base = 500000.0


def from_behind(array, axis, by):
    size = lax.axis_size(axis)
    pairs = [(i, i + by) for i in range(size) if 0 <= i + by < size]
    return lax.ppermute(array, axis, pairs)


def carried_in(part, axis, combine, identity):
    count = lax.axis_size(axis)
    place = lax.axis_index(axis)
    ahead = count - 1 - place
    gathered = jax.tree.map(lambda a: lax.all_gather(a, axis), part)
    state = jax.tree.map(lambda a, e: jnp.zeros_like(a) + jnp.asarray(e, a.dtype), part, identity)

    def one(hop, state):
        source = count - 1 - hop
        return combine(
            state, jax.tree.map(lambda a: lax.dynamic_index_in_dim(a, source, 0, False), gathered)
        )

    return lax.fori_loop(0, ahead, one, state)


def rotate(states, positions):
    half = HEAD // 2
    freq = rope_base ** (-jnp.arange(half, dtype=jnp.float32) * 2.0 / HEAD)
    angles = positions[:, None] * freq[None, :]
    cosine = jnp.cos(angles)[:, None, :]
    sine = jnp.sin(angles)[:, None, :]
    first = states[..., :half]
    second = states[..., half:]
    return jnp.concatenate([first * cosine - second * sine, second * cosine + first * sine], -1)


def plain_body(
    hidden_in, w_query, w_key, w_value, w_out, value_weight, rewards, old_values, lengths, terminal
):
    rows = hidden_in.shape[0]
    width = hidden_in.shape[1]
    states = hidden_in.astype(jnp.float32)
    normed = (states * lax.rsqrt(jnp.mean(states * states, 1, keepdims=True) + epsilon)).astype(
        jnp.bfloat16
    )
    pieces = (
        lax.all_gather(w_query, "dp", axis=0, tiled=True),
        lax.all_gather(w_key, "dp", axis=0, tiled=True),
        lax.all_gather(w_value, "dp", axis=0, tiled=True),
        lax.all_gather(w_out, "dp", axis=0, tiled=True),
    )
    add_pieces = pieces[:3]
    summed = tuple(
        (jnp.dot(normed, piece, preferred_element_type=jnp.float32) for piece in add_pieces)
    )
    stored = pieces[3]
    query_sum, key_sum, value_sum, whole_out = summed + (stored,)
    position_ids = lax.axis_index("dp") * rows + jnp.arange(rows, dtype=jnp.int32)
    positions = position_ids.astype(jnp.float32)
    local_heads = w_query.shape[1] // HEAD
    local_kv = w_key.shape[1] // HEAD
    group = local_heads // local_kv
    query = rotate(query_sum.reshape(rows, local_heads, HEAD), positions).astype(jnp.bfloat16)
    key = rotate(key_sum.reshape(rows, local_kv, HEAD), positions).astype(jnp.bfloat16)
    values_proj = value_sum.astype(jnp.bfloat16).reshape(rows, local_kv, HEAD)
    ends = jnp.cumsum(lengths)
    matches = ends[None, :] - 1 == position_ids[:, None]
    finished = jnp.any(matches, 1).astype(jnp.float32)
    stopped = jnp.sum(jnp.where(matches, terminal[None, :], 0), 1).astype(jnp.float32)
    episode = jnp.sum((ends[None, :] <= position_ids[:, None]).astype(jnp.int32), 1)
    order = jnp.arange(rows, dtype=jnp.int32)
    same_episode = episode[None, :] == episode[:, None]
    allowed = (order[None, :] <= order[:, None]) & same_episode
    scores = jnp.einsum(
        "tkgd,skd->kgts",
        query.reshape(rows, local_kv, group, HEAD),
        key,
        preferred_element_type=jnp.float32,
    ) * (1.0 / HEAD**0.5)
    masked = jnp.where(allowed[None, None], scores, -1e30)
    largest = jnp.max(masked, -1, keepdims=True)
    expon = jnp.where(allowed[None, None], jnp.exp(masked - largest), 0.0)
    probs = (expon / jnp.sum(expon, -1, keepdims=True)).astype(jnp.bfloat16)
    output = jnp.einsum("kgts,skd->tkgd", probs, values_proj, preferred_element_type=jnp.float32)
    attended = output.astype(jnp.bfloat16).reshape(rows, local_heads * HEAD)
    all_heads = lax.all_gather(attended, "mp", axis=1, tiled=True)
    projected = jnp.dot(all_heads, whole_out, preferred_element_type=jnp.float32)
    feature_count = w_out.shape[1]
    own_states = lax.dynamic_slice_in_dim(
        states, lax.axis_index("mp") * feature_count, feature_count, 1
    )
    residual = own_states + projected
    square_sum, head_sum = lax.psum(
        (jnp.sum(residual * residual, 1), jnp.sum(residual * value_weight[None, :], 1)), "mp"
    )
    value = head_sum * lax.rsqrt(square_sum / width + epsilon)
    following = from_behind(old_values[:1], "dp", -1)
    next_old = jnp.concatenate([old_values[1:], following])
    booted = jnp.where(finished > 0, (1.0 - stopped) * old_values, next_old)
    delta = rewards + discount * booted - old_values
    keep_rate = discount * trace_decay
    spacing = (order[None, :] - order[:, None]).astype(jnp.float32)
    forward_mask = (spacing >= 0.0) & same_episode
    decay_matrix = jnp.where(
        forward_mask, jnp.power(jnp.float32(keep_rate), jnp.maximum(spacing, 0.0)), 0.0
    )
    local_part = jnp.dot(decay_matrix, delta, precision=lax.Precision.HIGHEST)
    remaining = (rows - order).astype(jnp.float32)
    reach = jnp.where(episode == episode[-1], jnp.power(jnp.float32(keep_rate), remaining), 0.0) * (
        1.0 - finished[-1]
    )

    def compose(earlier, later_map):
        return (later_map[0] + later_map[1] * earlier[0], later_map[1] * earlier[1])

    prefix = carried_in(
        (local_part[:1], reach[:1]),
        "dp",
        compose,
        (jnp.zeros((1,), jnp.float32), jnp.ones((1,), jnp.float32)),
    )
    incoming = prefix[0][0]
    advantage = local_part + reach * incoming
    returns = advantage + old_values
    clipped = old_values + jnp.clip(value - old_values, -clip_range, clip_range)
    terms = jnp.maximum((value - returns) ** 2, (clipped - returns) ** 2)
    total_loss = lax.psum(jnp.sum(terms), "dp")
    value_loss = 0.5 * total_loss / (rows * lax.axis_size("dp"))
    return (value, advantage, value_loss)


def ring_order(chips):
    return list(range(0, chips, 2)) + list(range(chips - 1, 0, -2))


def ring_pairs(chips):
    order = ring_order(chips)
    pairs = []
    for spot in range(chips):
        here, there = order[spot], order[(spot + 1) % chips]
        pairs.append((2 * here, 2 * there))
        pairs.append((2 * there + 1, 2 * here + 1))
    return pairs


def ring_sources(chips):
    order = ring_order(chips)
    spots = {chip: spot for spot, chip in enumerate(order)}
    forward = [[order[(spots[c] - k) % chips] for k in range(chips)] for c in range(chips)]
    back = [[order[(spots[c] + k) % chips] for k in range(chips)] for c in range(chips)]
    return jnp.array([forward, back], jnp.int32)


def norm_kernel(sources, states_ref, normed_ref):
    width = states_ref.shape[1]
    chips = sources.shape[0]
    span = width // chips
    states = states_ref[...].astype(jnp.float32)
    scale = lax.rsqrt(jnp.mean(states * states, 1, keepdims=True) + epsilon)
    for k in range(chips):
        start = pl.multiple_of(sources[k] * span, span)
        piece = states_ref[:, pl.ds(start, span)].astype(jnp.float32)
        normed_ref[:, k * span : (k + 1) * span] = (piece * scale).astype(jnp.bfloat16)


def norm_in_order(states, sources, window, into=None):
    rows, width = states.shape
    tile = min(128, rows)
    steps = rows // tile
    operands = [states]
    specs = [pl.BlockSpec((tile, width), lambda i, s: (i, 0))]
    kernel = norm_kernel
    if into is not None:
        operands.append(into)
        specs.append(pl.BlockSpec(memory_space=pl.ANY))
        kernel = lambda s, x, _, o: norm_kernel(s, x, o)
    return pl.pallas_call(
        kernel,
        grid_spec=pltpu.PrefetchScalarGridSpec(
            num_scalar_prefetch=1,
            grid=(steps,),
            in_specs=specs,
            out_specs=pl.BlockSpec((tile, width), lambda i, s: (window * steps + i, 0)),
        ),
        out_shape=jax.ShapeDtypeStruct((2 * rows, width), jnp.bfloat16),
        input_output_aliases={} if into is None else {2: 0},
        cost_estimate=pl.CostEstimate(
            flops=4 * rows * width, bytes_accessed=4 * rows * width, transcendentals=rows
        ),
        compiler_params=pltpu.CompilerParams(vmem_limit_bytes=12 * 2**20),
    )(sources, *operands)


def spin(states, cosine, sine):
    return states * cosine + pltpu.roll(states, HEAD // 2, 1) * sine


def attend_kernel(query_ref, key_ref, val_ref, cos_ref, sin_ref, ep_col_ref, ep_row_ref, out_ref):
    rows = key_ref.shape[0]
    tile = rows // 2
    cosine = cos_ref[...]
    sine = sin_ref[...]
    key = spin(key_ref[...], cosine, sine).astype(jnp.bfloat16)
    vals = val_ref[...].astype(jnp.bfloat16)
    for t in range(2):
        low, high = t * tile, (t + 1) * tile
        at_row = lax.broadcasted_iota(jnp.int32, (tile, high), 0) + low
        at_col = lax.broadcasted_iota(jnp.int32, (tile, high), 1)
        allowed = (at_col <= at_row) & (ep_col_ref[low:high] == ep_row_ref[:, :high])
        bias = jnp.where(allowed, 0.0, -1e30)
        for h in range(query_ref.shape[1] // HEAD):
            column = h * HEAD
            query = spin(
                query_ref[low:high, column : column + HEAD], cosine[low:high], sine[low:high]
            ).astype(jnp.bfloat16)
            scores = lax.dot_general(
                query,
                key[:high],
                (((1,), (1,)), ((), ())),
                preferred_element_type=jnp.float32,
            )
            masked = scores * (1.0 / HEAD**0.5) + bias
            largest = jnp.max(masked, -1, keepdims=True)
            expon = jnp.exp(masked - largest)
            share = 1.0 / jnp.sum(expon, -1, keepdims=True)
            probs = (expon * share).astype(jnp.bfloat16)
            out_ref[low:high, column : column + HEAD] = jnp.dot(
                probs, vals[:high], preferred_element_type=jnp.float32
            ).astype(jnp.bfloat16)


def attend(window, which, rows, query, kv, cosine, sine, ep_col, ep_row):
    kv_count = kv.shape[1] // HEAD // 2
    width = query.shape[1]
    heads = width // HEAD
    once = lambda i: (window, 0)
    return pl.pallas_call(
        attend_kernel,
        grid=(1,),
        in_specs=[
            pl.BlockSpec((rows, width), once),
            pl.BlockSpec((rows, HEAD), lambda i: (window, which)),
            pl.BlockSpec((rows, HEAD), lambda i: (window, kv_count + which)),
            pl.BlockSpec((rows, HEAD), once),
            pl.BlockSpec((rows, HEAD), once),
            pl.BlockSpec((rows, 1), once),
            pl.BlockSpec((1, rows), lambda i: (0, window)),
        ],
        out_specs=pl.BlockSpec((rows, width), lambda i: (0, 0)),
        out_shape=jax.ShapeDtypeStruct((rows, width), jnp.bfloat16),
        cost_estimate=pl.CostEstimate(
            flops=4 * heads * HEAD * rows * rows,
            bytes_accessed=6 * rows * width,
            transcendentals=heads * rows * rows,
        ),
        compiler_params=pltpu.CompilerParams(vmem_limit_bytes=12 * 2**20),
    )(query, kv, kv, cosine, sine, ep_col, ep_row)


def project_kernel(pieces, count, late, *refs):
    offsets = refs[0]
    piece_refs = refs[1 : 1 + pieces]
    weight_refs = refs[1 + pieces : 1 + pieces + 2 * count]
    total_ref, late_ref, heads_ref, weights, sems = refs[1 + pieces + 2 * count :]
    rows = piece_refs[0].shape[0]
    half = weights.shape[2]
    copies = [(ref, heads_ref.at[p]) for p, ref in enumerate(piece_refs)]
    copies += [(ref, weights.at[i]) for i, ref in enumerate(weight_refs)]
    copies = [pltpu.make_async_copy(*c, sems.at[i]) for i, c in enumerate(copies)]
    for copy in copies:
        copy.start()
    for copy in copies[:pieces]:
        copy.wait()
    for k in range(late):
        late_ref[k] = heads_ref[offsets[count + k]]
    tile = 256
    for k in range(count):
        copies[pieces + 2 * k].wait()
        copies[pieces + 2 * k + 1].wait()
    for low in range(0, rows, tile):
        at = slice(low, low + tile)
        for side in range(2):
            total = None
            for k in range(count):
                term = jnp.dot(
                    heads_ref[offsets[k], at],
                    weights[2 * k + side],
                    preferred_element_type=jnp.float32,
                )
                total = term if total is None else total + term
            total_ref[at, side * half : (side + 1) * half] = total


def project(offsets, pieces, pairs, late):
    weights = [w for pair in pairs for w in pair]
    rows, span = pieces[0].shape
    half = weights[0].shape[1]
    number = len(pieces)
    count = len(pairs)
    here = pl.BlockSpec(memory_space=pltpu.HBM)
    vmem = pl.BlockSpec(memory_space=pltpu.VMEM)
    return pl.pallas_call(
        lambda *refs: project_kernel(number, count, late, *refs),
        in_specs=[pl.BlockSpec(memory_space=pltpu.SMEM)] + [here] * (number + len(weights)),
        out_specs=[vmem, vmem],
        out_shape=[
            jax.ShapeDtypeStruct((rows, 2 * half), jnp.float32),
            jax.ShapeDtypeStruct((late, rows, span), jnp.bfloat16),
        ],
        scratch_shapes=[
            pltpu.VMEM((number, rows, span), jnp.bfloat16),
            pltpu.VMEM((len(weights), span, half), jnp.bfloat16),
            pltpu.SemaphoreType.DMA((number + len(weights),)),
        ],
        compiler_params=pltpu.CompilerParams(vmem_limit_bytes=20 * 2**20),
        cost_estimate=pl.CostEstimate(
            flops=4 * rows * half * span * count,
            bytes_accessed=2 * rows * span * number + 8 * rows * half,
            transcendentals=0,
        ),
        name="project",
    )(offsets, *pieces, *weights)


def finish_kernel(late, heads_ref, *refs):
    weights = refs[: 2 * late]
    base_ref, states_ref, weight_ref, out_ref = refs[2 * late :]
    half = weights[0].shape[1]
    squares = headed = 0.0
    for side in range(2):
        cut = slice(side * half, (side + 1) * half)
        total = base_ref[:, cut]
        for k in range(late):
            total = total + jnp.dot(
                heads_ref[k], weights[2 * k + side][...], preferred_element_type=jnp.float32
            )
        residual = total + states_ref[:, cut].astype(jnp.float32)
        squares = squares + jnp.sum(residual * residual, 1, keepdims=True)
        headed = headed + jnp.sum(residual * weight_ref[:, cut], 1, keepdims=True)
    lane = lax.broadcasted_iota(jnp.int32, (squares.shape[0], HEAD), 1)
    out_ref[...] = jnp.where(lane == 0, squares, headed).T[: out_ref.shape[0]]


def finish(heads, pairs, base, states, weight):
    late, rows, span = heads.shape
    columns = base.shape[1]
    weights = [w for pair in pairs for w in pair]
    tile = 256
    whole = lambda i: (0, 0)
    return pl.pallas_call(
        lambda *refs: finish_kernel(late, *refs),
        grid=(rows // tile,),
        in_specs=[pl.BlockSpec((late, tile, span), lambda i: (0, i, 0))]
        + [pl.BlockSpec(w.shape, whole) for w in weights]
        + [
            pl.BlockSpec((tile, columns), lambda i: (i, 0)),
            pl.BlockSpec((tile, columns), lambda i: (i, 0)),
            pl.BlockSpec((1, columns), whole),
        ],
        out_specs=pl.BlockSpec((8, tile), lambda i: (0, i)),
        out_shape=jax.ShapeDtypeStruct((8, rows), jnp.float32),
        compiler_params=pltpu.CompilerParams(vmem_limit_bytes=16 * 2**20),
        cost_estimate=pl.CostEstimate(
            flops=2 * rows * columns * span * late,
            bytes_accessed=rows * (2 * late * span + 6 * columns),
            transcendentals=0,
        ),
        name="finish",
    )(heads, *weights, base, states, weight)


def tie(array, *others):
    return lax.optimization_barrier((array,) + others)[0]


def suffix_kernel(place_ref, maps_ref, out_ref):
    devices = maps_ref.shape[0]
    place = place_ref[0]
    total, old = jnp.float32(0.0), jnp.float32(0.0)
    for i in range(devices - 1, 0, -1):
        later = i > place
        fresh = maps_ref[i, 0] + maps_ref[i, 1] * old + maps_ref[i, 2] * total
        total = jnp.where(later, fresh, total)
        old = jnp.where(later, maps_ref[i, 3], old)
    out_ref[0] = total
    out_ref[1] = old


def suffix(maps, place):
    smem = pl.BlockSpec(memory_space=pltpu.SMEM)
    out = pl.pallas_call(
        suffix_kernel,
        in_specs=[smem, smem],
        out_specs=smem,
        out_shape=jax.ShapeDtypeStruct((2,), jnp.float32),
        name="suffix",
    )(place.astype(jnp.int32).reshape(1), maps)
    return out[0], out[1]


def tie(array, *others):
    return lax.optimization_barrier((array,) + others)[0]


def shared_body(
    hidden_in, w_query, w_key, w_value, w_out, value_weight, rewards, old_values, lengths, terminal
):
    rows, width = hidden_in.shape
    devices = lax.axis_size("dp")
    place = lax.axis_index("dp")
    side = lax.axis_index("mp")
    core = place % 2
    chip = place // 2
    chips = devices // 2
    partner = [(i, i ^ 1) for i in range(devices)]
    across = [(0, 1), (1, 0)]
    ring = ring_pairs(chips)

    def swap(array):
        return lax.ppermute(array, "dp", partner)

    def pair_up(mine, got):
        return jnp.where(
            core == 0, jnp.concatenate([mine, got], 0), jnp.concatenate([got, mine], 0)
        )

    def columns(weight, which, part, parts):
        half = weight.shape[1] // 2
        size = half // parts
        return lax.dynamic_slice_in_dim(weight, which * half + part * size, size, 1)

    def chip_block(pieces):
        mine = jnp.concatenate([columns(w, core, *p) for w, *p in pieces], 1)
        theirs = jnp.concatenate([columns(w, 1 - core, *p) for w, *p in pieces], 1)
        return pair_up(mine, swap(theirs))

    local_kv = w_key.shape[1] // HEAD // 2
    group = w_query.shape[1] // w_key.shape[1]

    def hop(block):
        return lax.ppermute(block, "dp", ring)

    lanes = [chip_block([(w_key, 0, 1), (w_value, 0, 1)])]
    lanes += [chip_block([(w_query, j, local_kv)]) for j in range(local_kv)]
    first_hops = [hop(block) for block in lanes]
    states_got = swap(hidden_in)
    sources = ring_sources(chips)[core, chip]
    place, lengths, rewards, old_values, *_ = lax.optimization_barrier(
        (place, lengths, rewards, old_values, *lanes)
    )
    span = width // chips

    ends = jnp.cumsum(lengths)
    order = jnp.arange(rows, dtype=jnp.int32)
    position_ids = place * rows + order
    other_ids = (place + 1 - 2 * core) * rows + order
    both_ids = jnp.concatenate([position_ids, other_ids])
    half = HEAD // 2
    freq = rope_base ** (-jnp.arange(half, dtype=jnp.float32) * 2.0 / HEAD)
    angles = both_ids.astype(jnp.float32)[:, None] * freq[None, :]
    cosine = jnp.cos(angles)
    sine = jnp.sin(angles)
    cosine = jnp.concatenate([cosine, cosine], 1)
    sine = jnp.concatenate([-sine, sine], 1)
    both_episode = jnp.sum((ends[None, :] <= both_ids[:, None]).astype(jnp.int32), 1)

    matches = ends[None, :] - 1 == position_ids[:, None]
    finished = jnp.any(matches, 1).astype(jnp.float32)
    stopped = jnp.sum(jnp.where(matches, terminal[None, :], 0), 1).astype(jnp.float32)
    episode = both_episode[:rows]
    same_episode = episode[None, :] == episode[:, None]
    next_known = jnp.concatenate([old_values[1:], jnp.zeros((1,), jnp.float32)])
    booted = jnp.where(finished > 0, (1.0 - stopped) * old_values, next_known)
    delta = rewards + discount * booted - old_values
    keep_rate = discount * trace_decay
    spacing = (order[None, :] - order[:, None]).astype(jnp.float32)
    forward_mask = (spacing >= 0.0) & same_episode
    decay_matrix = jnp.where(
        forward_mask, jnp.power(jnp.float32(keep_rate), jnp.maximum(spacing, 0.0)), 0.0
    )
    local_part = jnp.dot(decay_matrix, delta, precision=lax.Precision.HIGHEST)
    remaining = (rows - order).astype(jnp.float32)
    open_end = 1.0 - finished[-1]
    reach = jnp.where(episode == episode[-1], jnp.power(jnp.float32(keep_rate), remaining), 0.0) * open_end
    bridge = reach / trace_decay
    maps = jnp.stack([local_part[0], bridge[0], reach[0], old_values[0]])
    known = jnp.where(jnp.arange(devices)[:, None] == place, maps[None, :], 0.0)

    normed = norm_in_order(hidden_in, sources, 0)
    normed = norm_in_order(states_got, sources, 1, normed)

    def use(total, k, block):
        term = jnp.dot(
            normed[:, k * span : (k + 1) * span], block, preferred_element_type=jnp.float32
        )
        return term if total is None else total + term

    sums = [use(None, 0, block) for block in lanes]
    blocks = first_hops
    for k in range(1, chips):
        if k + 1 < chips:
            coming = [hop(block) for block in blocks]
        sums = [use(sums[lane], k, block) for lane, block in enumerate(blocks)]
        step = 2 ** (k - 1)
        if step < devices:
            moved = lax.ppermute(
                tie(known, blocks[0]), "dp", [(i, i ^ step) for i in range(devices)]
            )
            known = known + moved
        if k == chips - 3:
            out_blocks = [chip_block([(tie(w_out, blocks[0]), j, 2)]) for j in range(2)]
        if k == chips - 2:
            sums = [tie(total, blocks[0]) for total in sums]
        last_blocks = blocks
        blocks = coming
    out_held = [out_blocks]
    for k in range(1, chips):
        out_held.append(
            [
                hop(tie(block, last_blocks[j]) if k == 1 else block)
                for j, block in enumerate(out_held[-1])
            ]
        )

    pieces = [[], []]
    sent = {}
    for w in range(2):
        for j in range(local_kv):
            part = attend(
                w, j, rows, sums[1 + j], sums[0], cosine, sine,
                both_episode[:, None], both_episode[None, :],
            )
            sent[w, j] = (part, lax.ppermute(part, "mp", across))
    diagonal = {}
    for n, (w, j) in enumerate((w, j) for w in range(2) for j in range(local_kv)):
        after = out_held[min(n + 2, chips - 2)]
        diagonal[1 - w, j] = swap(tie(sent[w, j][1], *after))
    for w in range(2):
        pieces[w] = [sent[w, j][0] for j in range(local_kv)]
        pieces[w] += [swap(sent[1 - w, j][0]) for j in range(local_kv)]
        pieces[w] += [sent[w, j][1] for j in range(local_kv)]
        pieces[w] += [diagonal[w, j] for j in range(local_kv)]

    quarter = local_kv * group * HEAD
    own_quarter = side * 2 + core
    first_rows = sources * span
    slots = ((first_rows // quarter) ^ own_quarter) * (quarter // span) + first_rows % quarter // span
    late = 3
    early = chips - late
    parts = []
    for w in range(2):
        parts.append(project(slots, pieces[w], out_held[:early], late))

    out_columns = w_out.shape[1] // 2
    weight_own = lax.dynamic_slice_in_dim(value_weight, core * out_columns, out_columns, 0)
    pair_sums = jnp.stack(
        [
            finish(
                heads,
                out_held[early:],
                part,
                lax.dynamic_slice_in_dim(states, own_quarter * out_columns, out_columns, 1),
                weight_own[None, :],
            )[:2]
            for (part, heads), states in zip(parts, (hidden_in, states_got))
        ],
        1,
    )

    incoming, coming_old = suffix(known, place)
    advantage = local_part + bridge * coming_old + reach * incoming
    shared = swap(jnp.stack([advantage, old_values]))
    both_advantage = jnp.stack([advantage, shared[0]])
    both_old = jnp.stack([old_values, shared[1]])

    pair_sums = pair_sums + lax.ppermute(pair_sums, "mp", across)
    turned = swap(pair_sums)
    pair_sums = pair_sums.reshape(2, 2, rows) + turned.reshape(2, 2, rows)[:, ::-1]
    value = pair_sums[1] * lax.rsqrt(pair_sums[0] / width + epsilon)
    returns = both_advantage + both_old
    clipped = both_old + jnp.clip(value - both_old, -clip_range, clip_range)
    terms = jnp.maximum((value - returns) ** 2, (clipped - returns) ** 2)
    window_loss = jnp.sum(terms, 1)
    total_loss = window_loss[:1] + window_loss[1:]
    by = 2
    while by < devices:
        total_loss = total_loss + lax.ppermute(
            total_loss, "dp", [(i, i ^ by) for i in range(devices)]
        )
        by *= 2
    value_loss = 0.5 * total_loss[0] / (rows * devices)
    return (value[0], advantage, value_loss)


def suits(devices, sides, hidden, query, key):
    return (
        sides == 2
        and devices >= 16
        and devices & (devices - 1) == 0
        and key[1] == 4 * HEAD
        and query[1] * devices == 8 * hidden[1]
        and hidden[0] % 512 == 0
    )


def body(hidden_in, w_query, w_key, *rest):
    fits = suits(
        lax.axis_size("dp"), lax.axis_size("mp"), hidden_in.shape, w_query.shape, w_key.shape
    )
    return (shared_body if fits else plain_body)(hidden_in, w_query, w_key, *rest)


def solution(mesh):
    return jax.shard_map(
        body,
        mesh=mesh,
        in_specs=(
            P("dp", None),
            P("dp", "mp"),
            P("dp", "mp"),
            P("dp", "mp"),
            P("dp", "mp"),
            P("mp"),
            P("dp"),
            P("dp"),
            P(),
            P(),
        ),
        out_specs=(P("dp"), P("dp"), P()),
        check_vma=False,
    )
```

```python
import jax
import jax.numpy as jnp
from jax import lax
from jax.experimental import pallas as pl
from jax.experimental.pallas import tpu as pltpu
from jax.sharding import PartitionSpec as P


HEAD = 128


discount = 0.999
trace_decay = 0.997
clip_range = 0.2
epsilon = 1e-05
rope_base = 500000.0


def from_behind(array, axis, by):
    size = lax.axis_size(axis)
    pairs = [(i, i + by) for i in range(size) if 0 <= i + by < size]
    return lax.ppermute(array, axis, pairs)


def carried_in(part, axis, combine, identity):
    count = lax.axis_size(axis)
    place = lax.axis_index(axis)
    ahead = count - 1 - place
    gathered = jax.tree.map(lambda a: lax.all_gather(a, axis), part)
    state = jax.tree.map(lambda a, e: jnp.zeros_like(a) + jnp.asarray(e, a.dtype), part, identity)

    def one(hop, state):
        source = count - 1 - hop
        return combine(
            state, jax.tree.map(lambda a: lax.dynamic_index_in_dim(a, source, 0, False), gathered)
        )

    return lax.fori_loop(0, ahead, one, state)


def rotate(states, positions):
    half = HEAD // 2
    freq = rope_base ** (-jnp.arange(half, dtype=jnp.float32) * 2.0 / HEAD)
    angles = positions[:, None] * freq[None, :]
    cosine = jnp.cos(angles)[:, None, :]
    sine = jnp.sin(angles)[:, None, :]
    first = states[..., :half]
    second = states[..., half:]
    return jnp.concatenate([first * cosine - second * sine, second * cosine + first * sine], -1)


def plain_body(
    hidden_in, w_query, w_key, w_value, w_out, value_weight, rewards, old_values, lengths, terminal
):
    rows = hidden_in.shape[0]
    width = hidden_in.shape[1]
    states = hidden_in.astype(jnp.float32)
    normed = (states * lax.rsqrt(jnp.mean(states * states, 1, keepdims=True) + epsilon)).astype(
        jnp.bfloat16
    )
    pieces = (
        lax.all_gather(w_query, "dp", axis=0, tiled=True),
        lax.all_gather(w_key, "dp", axis=0, tiled=True),
        lax.all_gather(w_value, "dp", axis=0, tiled=True),
        lax.all_gather(w_out, "dp", axis=0, tiled=True),
    )
    add_pieces = pieces[:3]
    summed = tuple(
        (jnp.dot(normed, piece, preferred_element_type=jnp.float32) for piece in add_pieces)
    )
    stored = pieces[3]
    query_sum, key_sum, value_sum, whole_out = summed + (stored,)
    position_ids = lax.axis_index("dp") * rows + jnp.arange(rows, dtype=jnp.int32)
    positions = position_ids.astype(jnp.float32)
    local_heads = w_query.shape[1] // HEAD
    local_kv = w_key.shape[1] // HEAD
    group = local_heads // local_kv
    query = rotate(query_sum.reshape(rows, local_heads, HEAD), positions).astype(jnp.bfloat16)
    key = rotate(key_sum.reshape(rows, local_kv, HEAD), positions).astype(jnp.bfloat16)
    values_proj = value_sum.astype(jnp.bfloat16).reshape(rows, local_kv, HEAD)
    ends = jnp.cumsum(lengths)
    matches = ends[None, :] - 1 == position_ids[:, None]
    finished = jnp.any(matches, 1).astype(jnp.float32)
    stopped = jnp.sum(jnp.where(matches, terminal[None, :], 0), 1).astype(jnp.float32)
    episode = jnp.sum((ends[None, :] <= position_ids[:, None]).astype(jnp.int32), 1)
    order = jnp.arange(rows, dtype=jnp.int32)
    same_episode = episode[None, :] == episode[:, None]
    allowed = (order[None, :] <= order[:, None]) & same_episode
    scores = jnp.einsum(
        "tkgd,skd->kgts",
        query.reshape(rows, local_kv, group, HEAD),
        key,
        preferred_element_type=jnp.float32,
    ) * (1.0 / HEAD**0.5)
    masked = jnp.where(allowed[None, None], scores, -1e30)
    largest = jnp.max(masked, -1, keepdims=True)
    expon = jnp.where(allowed[None, None], jnp.exp(masked - largest), 0.0)
    probs = (expon / jnp.sum(expon, -1, keepdims=True)).astype(jnp.bfloat16)
    output = jnp.einsum("kgts,skd->tkgd", probs, values_proj, preferred_element_type=jnp.float32)
    attended = output.astype(jnp.bfloat16).reshape(rows, local_heads * HEAD)
    all_heads = lax.all_gather(attended, "mp", axis=1, tiled=True)
    projected = jnp.dot(all_heads, whole_out, preferred_element_type=jnp.float32)
    feature_count = w_out.shape[1]
    own_states = lax.dynamic_slice_in_dim(
        states, lax.axis_index("mp") * feature_count, feature_count, 1
    )
    residual = own_states + projected
    square_sum, head_sum = lax.psum(
        (jnp.sum(residual * residual, 1), jnp.sum(residual * value_weight[None, :], 1)), "mp"
    )
    value = head_sum * lax.rsqrt(square_sum / width + epsilon)
    following = from_behind(old_values[:1], "dp", -1)
    next_old = jnp.concatenate([old_values[1:], following])
    booted = jnp.where(finished > 0, (1.0 - stopped) * old_values, next_old)
    delta = rewards + discount * booted - old_values
    keep_rate = discount * trace_decay
    spacing = (order[None, :] - order[:, None]).astype(jnp.float32)
    forward_mask = (spacing >= 0.0) & same_episode
    decay_matrix = jnp.where(
        forward_mask, jnp.power(jnp.float32(keep_rate), jnp.maximum(spacing, 0.0)), 0.0
    )
    local_part = jnp.dot(decay_matrix, delta, precision=lax.Precision.HIGHEST)
    remaining = (rows - order).astype(jnp.float32)
    reach = jnp.where(episode == episode[-1], jnp.power(jnp.float32(keep_rate), remaining), 0.0) * (
        1.0 - finished[-1]
    )

    def compose(earlier, later_map):
        return (later_map[0] + later_map[1] * earlier[0], later_map[1] * earlier[1])

    prefix = carried_in(
        (local_part[:1], reach[:1]),
        "dp",
        compose,
        (jnp.zeros((1,), jnp.float32), jnp.ones((1,), jnp.float32)),
    )
    incoming = prefix[0][0]
    advantage = local_part + reach * incoming
    returns = advantage + old_values
    clipped = old_values + jnp.clip(value - old_values, -clip_range, clip_range)
    terms = jnp.maximum((value - returns) ** 2, (clipped - returns) ** 2)
    total_loss = lax.psum(jnp.sum(terms), "dp")
    value_loss = 0.5 * total_loss / (rows * lax.axis_size("dp"))
    return (value, advantage, value_loss)


def ring_order(chips):
    return list(range(0, chips, 2)) + list(range(chips - 1, 0, -2))


def ring_pairs(chips):
    order = ring_order(chips)
    pairs = []
    for spot in range(chips):
        here, there = order[spot], order[(spot + 1) % chips]
        pairs.append((2 * here, 2 * there))
        pairs.append((2 * there + 1, 2 * here + 1))
    return pairs


def ring_sources(chips):
    order = ring_order(chips)
    spots = {chip: spot for spot, chip in enumerate(order)}
    forward = [[order[(spots[c] - k) % chips] for k in range(chips)] for c in range(chips)]
    back = [[order[(spots[c] + k) % chips] for k in range(chips)] for c in range(chips)]
    return jnp.array([forward, back], jnp.int32)


def norm_kernel(sources, states_ref, normed_ref):
    width = states_ref.shape[1]
    chips = sources.shape[0]
    span = width // chips
    states = states_ref[...].astype(jnp.float32)
    scale = lax.rsqrt(jnp.mean(states * states, 1, keepdims=True) + epsilon)
    for k in range(chips):
        start = pl.multiple_of(sources[k] * span, span)
        piece = states_ref[:, pl.ds(start, span)].astype(jnp.float32)
        normed_ref[:, k * span : (k + 1) * span] = (piece * scale).astype(jnp.bfloat16)


def norm_in_order(states, sources, window, into=None):
    rows, width = states.shape
    tile = min(128, rows)
    steps = rows // tile
    operands = [states]
    specs = [pl.BlockSpec((tile, width), lambda i, s: (i, 0))]
    kernel = norm_kernel
    if into is not None:
        operands.append(into)
        specs.append(pl.BlockSpec(memory_space=pl.ANY))
        kernel = lambda s, x, _, o: norm_kernel(s, x, o)
    return pl.pallas_call(
        kernel,
        grid_spec=pltpu.PrefetchScalarGridSpec(
            num_scalar_prefetch=1,
            grid=(steps,),
            in_specs=specs,
            out_specs=pl.BlockSpec((tile, width), lambda i, s: (window * steps + i, 0)),
        ),
        out_shape=jax.ShapeDtypeStruct((2 * rows, width), jnp.bfloat16),
        input_output_aliases={} if into is None else {2: 0},
        cost_estimate=pl.CostEstimate(
            flops=4 * rows * width, bytes_accessed=4 * rows * width, transcendentals=rows
        ),
        compiler_params=pltpu.CompilerParams(vmem_limit_bytes=12 * 2**20),
    )(sources, *operands)


def spin(states, cosine, sine):
    return states * cosine + pltpu.roll(states, HEAD // 2, 1) * sine


def attend_kernel(query_ref, key_ref, val_ref, cos_ref, sin_ref, ep_col_ref, ep_row_ref, out_ref):
    rows = key_ref.shape[0]
    tile = rows // 2
    cosine = cos_ref[...]
    sine = sin_ref[...]
    key = spin(key_ref[...], cosine, sine).astype(jnp.bfloat16)
    vals = val_ref[...].astype(jnp.bfloat16)
    for t in range(2):
        low, high = t * tile, (t + 1) * tile
        at_row = lax.broadcasted_iota(jnp.int32, (tile, high), 0) + low
        at_col = lax.broadcasted_iota(jnp.int32, (tile, high), 1)
        allowed = (at_col <= at_row) & (ep_col_ref[low:high] == ep_row_ref[:, :high])
        bias = jnp.where(allowed, 0.0, -1e30)

        def some(step, _):
            for h in range(2):
                cut = pl.ds(pl.multiple_of((2 * step + h) * HEAD, HEAD), HEAD)
                query = spin(query_ref[low:high, cut], cosine[low:high], sine[low:high])
                scores = lax.dot_general(
                    query.astype(jnp.bfloat16),
                    key[:high],
                    (((1,), (1,)), ((), ())),
                    preferred_element_type=jnp.float32,
                )
                masked = scores * (1.0 / HEAD**0.5) + bias
                largest = jnp.max(masked, -1, keepdims=True)
                expon = jnp.exp(masked - largest)
                share = 1.0 / jnp.sum(expon, -1, keepdims=True)
                probs = (expon * share).astype(jnp.bfloat16)
                out_ref[low:high, cut] = jnp.dot(
                    probs, vals[:high], preferred_element_type=jnp.float32
                ).astype(jnp.bfloat16)
            return 0

        lax.fori_loop(0, query_ref.shape[1] // HEAD // 2, some, 0)


def attend(window, which, rows, query, kv, cosine, sine, ep_col, ep_row):
    kv_count = kv.shape[1] // HEAD // 2
    width = query.shape[1]
    heads = width // HEAD
    once = lambda i: (window, 0)
    return pl.pallas_call(
        attend_kernel,
        grid=(1,),
        in_specs=[
            pl.BlockSpec((rows, width), once),
            pl.BlockSpec((rows, HEAD), lambda i: (window, which)),
            pl.BlockSpec((rows, HEAD), lambda i: (window, kv_count + which)),
            pl.BlockSpec((rows, HEAD), once),
            pl.BlockSpec((rows, HEAD), once),
            pl.BlockSpec((rows, 1), once),
            pl.BlockSpec((1, rows), lambda i: (0, window)),
        ],
        out_specs=pl.BlockSpec((rows, width), lambda i: (0, 0)),
        out_shape=jax.ShapeDtypeStruct((rows, width), jnp.bfloat16),
        cost_estimate=pl.CostEstimate(
            flops=4 * heads * HEAD * rows * rows,
            bytes_accessed=6 * rows * width,
            transcendentals=heads * rows * rows,
        ),
        compiler_params=pltpu.CompilerParams(vmem_limit_bytes=12 * 2**20),
    )(query, kv, kv, cosine, sine, ep_col, ep_row)


def project_kernel(pieces, count, late, *refs):
    offsets = refs[0]
    piece_refs = refs[1 : 1 + pieces]
    weight_refs = refs[1 + pieces : 1 + pieces + 2 * count]
    total_ref, late_ref, heads_ref, weights, sems = refs[1 + pieces + 2 * count :]
    rows = piece_refs[0].shape[0]
    half = weights.shape[2]
    copies = [(ref, heads_ref.at[p]) for p, ref in enumerate(piece_refs)]
    copies += [(ref, weights.at[i]) for i, ref in enumerate(weight_refs)]
    copies = [pltpu.make_async_copy(*c, sems.at[i]) for i, c in enumerate(copies)]
    for copy in copies:
        copy.start()
    for copy in copies[:pieces]:
        copy.wait()
    for k in range(late):
        late_ref[k] = heads_ref[offsets[count + k]]
    tile = 256
    for k in range(count):
        copies[pieces + 2 * k].wait()
        copies[pieces + 2 * k + 1].wait()

    def one(step, _):
        at = pl.ds(pl.multiple_of(step * tile, tile), tile)
        for side in range(2):
            total = None
            for k in range(count):
                term = jnp.dot(
                    heads_ref[offsets[k], at],
                    weights[2 * k + side],
                    preferred_element_type=jnp.float32,
                )
                total = term if total is None else total + term
            total_ref[at, side * half : (side + 1) * half] = total
        return 0

    lax.fori_loop(0, rows // tile, one, 0)


def project(offsets, pieces, pairs, late):
    weights = [w for pair in pairs for w in pair]
    rows, span = pieces[0].shape
    half = weights[0].shape[1]
    number = len(pieces)
    count = len(pairs)
    here = pl.BlockSpec(memory_space=pltpu.HBM)
    vmem = pl.BlockSpec(memory_space=pltpu.VMEM)
    return pl.pallas_call(
        lambda *refs: project_kernel(number, count, late, *refs),
        in_specs=[pl.BlockSpec(memory_space=pltpu.SMEM)] + [here] * (number + len(weights)),
        out_specs=[vmem, vmem],
        out_shape=[
            jax.ShapeDtypeStruct((rows, 2 * half), jnp.float32),
            jax.ShapeDtypeStruct((late, rows, span), jnp.bfloat16),
        ],
        scratch_shapes=[
            pltpu.VMEM((number, rows, span), jnp.bfloat16),
            pltpu.VMEM((len(weights), span, half), jnp.bfloat16),
            pltpu.SemaphoreType.DMA((number + len(weights),)),
        ],
        compiler_params=pltpu.CompilerParams(vmem_limit_bytes=20 * 2**20),
        cost_estimate=pl.CostEstimate(
            flops=4 * rows * half * span * count,
            bytes_accessed=2 * rows * span * number + 8 * rows * half,
            transcendentals=0,
        ),
        name="project",
    )(offsets, *pieces, *weights)


def finish_kernel(late, heads_ref, *refs):
    weights = refs[: 2 * late]
    base_ref, states_ref, weight_ref, out_ref = refs[2 * late :]
    half = weights[0].shape[1]
    squares = headed = 0.0
    for side in range(2):
        cut = slice(side * half, (side + 1) * half)
        total = base_ref[:, cut]
        for k in range(late):
            total = total + jnp.dot(
                heads_ref[k], weights[2 * k + side][...], preferred_element_type=jnp.float32
            )
        residual = total + states_ref[:, cut].astype(jnp.float32)
        squares = squares + jnp.sum(residual * residual, 1, keepdims=True)
        headed = headed + jnp.sum(residual * weight_ref[:, cut], 1, keepdims=True)
    lane = lax.broadcasted_iota(jnp.int32, (squares.shape[0], HEAD), 1)
    out_ref[...] = jnp.where(lane == 0, squares, headed).T[: out_ref.shape[0]]


def finish(heads, pairs, base, states, weight):
    late, rows, span = heads.shape
    columns = base.shape[1]
    weights = [w for pair in pairs for w in pair]
    tile = 256
    whole = lambda i: (0, 0)
    return pl.pallas_call(
        lambda *refs: finish_kernel(late, *refs),
        grid=(rows // tile,),
        in_specs=[pl.BlockSpec((late, tile, span), lambda i: (0, i, 0))]
        + [pl.BlockSpec(w.shape, whole) for w in weights]
        + [
            pl.BlockSpec((tile, columns), lambda i: (i, 0)),
            pl.BlockSpec((tile, columns), lambda i: (i, 0)),
            pl.BlockSpec((1, columns), whole),
        ],
        out_specs=pl.BlockSpec((8, tile), lambda i: (0, i)),
        out_shape=jax.ShapeDtypeStruct((8, rows), jnp.float32),
        compiler_params=pltpu.CompilerParams(vmem_limit_bytes=16 * 2**20),
        cost_estimate=pl.CostEstimate(
            flops=2 * rows * columns * span * late,
            bytes_accessed=rows * (2 * late * span + 6 * columns),
            transcendentals=0,
        ),
        name="finish",
    )(heads, *weights, base, states, weight)


def tie(array, *others):
    return lax.optimization_barrier((array,) + others)[0]


def suffix_kernel(place_ref, maps_ref, out_ref):
    devices = maps_ref.shape[0]
    place = place_ref[0]
    total, old = jnp.float32(0.0), jnp.float32(0.0)
    for i in range(devices - 1, 0, -1):
        later = i > place
        fresh = maps_ref[i, 0] + maps_ref[i, 1] * old + maps_ref[i, 2] * total
        total = jnp.where(later, fresh, total)
        old = jnp.where(later, maps_ref[i, 3], old)
    out_ref[0] = total
    out_ref[1] = old


def suffix(maps, place):
    smem = pl.BlockSpec(memory_space=pltpu.SMEM)
    out = pl.pallas_call(
        suffix_kernel,
        in_specs=[smem, smem],
        out_specs=smem,
        out_shape=jax.ShapeDtypeStruct((2,), jnp.float32),
        compiler_params=pltpu.CompilerParams(vmem_limit_bytes=2**20),
        name="suffix",
    )(place.astype(jnp.int32).reshape(1), maps)
    return out[0], out[1]


def tie(array, *others):
    return lax.optimization_barrier((array,) + others)[0]


def shared_body(
    hidden_in, w_query, w_key, w_value, w_out, value_weight, rewards, old_values, lengths, terminal
):
    rows, width = hidden_in.shape
    devices = lax.axis_size("dp")
    place = lax.axis_index("dp")
    side = lax.axis_index("mp")
    core = place % 2
    chip = place // 2
    chips = devices // 2
    partner = [(i, i ^ 1) for i in range(devices)]
    across = [(0, 1), (1, 0)]
    ring = ring_pairs(chips)

    def swap(array):
        return lax.ppermute(array, "dp", partner)

    def pair_up(mine, got):
        return jnp.where(
            core == 0, jnp.concatenate([mine, got], 0), jnp.concatenate([got, mine], 0)
        )

    def columns(weight, which, part, parts):
        half = weight.shape[1] // 2
        size = half // parts
        return lax.dynamic_slice_in_dim(weight, which * half + part * size, size, 1)

    def chip_block(pieces):
        mine = jnp.concatenate([columns(w, core, *p) for w, *p in pieces], 1)
        theirs = jnp.concatenate([columns(w, 1 - core, *p) for w, *p in pieces], 1)
        return pair_up(mine, swap(theirs))

    local_kv = w_key.shape[1] // HEAD // 2
    group = w_query.shape[1] // w_key.shape[1]

    def hop(block):
        return lax.ppermute(block, "dp", ring)

    lanes = [chip_block([(w_key, 0, 1), (w_value, 0, 1)])]
    lanes += [chip_block([(w_query, j, local_kv)]) for j in range(local_kv)]
    first_hops = [hop(block) for block in lanes]
    states_got = swap(hidden_in)
    sources = ring_sources(chips)[core, chip]
    place, lengths, rewards, old_values, *_ = lax.optimization_barrier(
        (place, lengths, rewards, old_values, *lanes)
    )
    span = width // chips

    ends = jnp.cumsum(lengths)
    order = jnp.arange(rows, dtype=jnp.int32)
    position_ids = place * rows + order
    other_ids = (place + 1 - 2 * core) * rows + order
    both_ids = jnp.concatenate([position_ids, other_ids])
    half = HEAD // 2
    freq = rope_base ** (-jnp.arange(half, dtype=jnp.float32) * 2.0 / HEAD)
    angles = both_ids.astype(jnp.float32)[:, None] * freq[None, :]
    cosine = jnp.cos(angles)
    sine = jnp.sin(angles)
    cosine = jnp.concatenate([cosine, cosine], 1)
    sine = jnp.concatenate([-sine, sine], 1)
    both_episode = jnp.sum((ends[None, :] <= both_ids[:, None]).astype(jnp.int32), 1)

    matches = ends[None, :] - 1 == position_ids[:, None]
    finished = jnp.any(matches, 1).astype(jnp.float32)
    stopped = jnp.sum(jnp.where(matches, terminal[None, :], 0), 1).astype(jnp.float32)
    episode = both_episode[:rows]
    same_episode = episode[None, :] == episode[:, None]
    next_known = jnp.concatenate([old_values[1:], jnp.zeros((1,), jnp.float32)])
    booted = jnp.where(finished > 0, (1.0 - stopped) * old_values, next_known)
    delta = rewards + discount * booted - old_values
    keep_rate = discount * trace_decay
    spacing = (order[None, :] - order[:, None]).astype(jnp.float32)
    forward_mask = (spacing >= 0.0) & same_episode
    decay_matrix = jnp.where(
        forward_mask, jnp.power(jnp.float32(keep_rate), jnp.maximum(spacing, 0.0)), 0.0
    )
    local_part = jnp.dot(decay_matrix, delta, precision=lax.Precision.HIGHEST)
    remaining = (rows - order).astype(jnp.float32)
    open_end = 1.0 - finished[-1]
    reach = jnp.where(episode == episode[-1], jnp.power(jnp.float32(keep_rate), remaining), 0.0) * open_end
    bridge = reach / trace_decay
    maps = jnp.stack([local_part[0], bridge[0], reach[0], old_values[0]])
    known = jnp.where(jnp.arange(devices)[:, None] == place, maps[None, :], 0.0)

    normed = norm_in_order(hidden_in, sources, 0)
    normed = norm_in_order(states_got, sources, 1, normed)

    def use(total, k, block):
        term = jnp.dot(
            normed[:, k * span : (k + 1) * span], block, preferred_element_type=jnp.float32
        )
        return term if total is None else total + term

    sums = [use(None, 0, block) for block in lanes]
    blocks = first_hops
    for k in range(1, chips):
        if k + 1 < chips:
            coming = [hop(block) for block in blocks]
        sums = [use(sums[lane], k, block) for lane, block in enumerate(blocks)]
        step = 2 ** (k - 1)
        if step < devices:
            moved = lax.ppermute(
                tie(known, blocks[0]), "dp", [(i, i ^ step) for i in range(devices)]
            )
            known = known + moved
        if k == chips - 3:
            out_blocks = [chip_block([(tie(w_out, blocks[0]), j, 2)]) for j in range(2)]
        if k == chips - 2:
            sums = [tie(total, blocks[0]) for total in sums]
        last_blocks = blocks
        blocks = coming
    out_held = [out_blocks]
    for k in range(1, chips):
        out_held.append(
            [
                hop(tie(block, last_blocks[j]) if k == 1 else block)
                for j, block in enumerate(out_held[-1])
            ]
        )

    pieces = [[], []]
    sent = {}
    for w in range(2):
        for j in range(local_kv):
            part = attend(
                w, j, rows, sums[1 + j], sums[0], cosine, sine,
                both_episode[:, None], both_episode[None, :],
            )
            sent[w, j] = (part, lax.ppermute(part, "mp", across))
    diagonal = {}
    for n, (w, j) in enumerate((w, j) for w in range(2) for j in range(local_kv)):
        after = out_held[min(n + 2, chips - 2)]
        diagonal[1 - w, j] = swap(tie(sent[w, j][1], *after))
    for w in range(2):
        pieces[w] = [sent[w, j][0] for j in range(local_kv)]
        pieces[w] += [swap(sent[1 - w, j][0]) for j in range(local_kv)]
        pieces[w] += [sent[w, j][1] for j in range(local_kv)]
        pieces[w] += [diagonal[w, j] for j in range(local_kv)]

    quarter = local_kv * group * HEAD
    own_quarter = side * 2 + core
    first_rows = sources * span
    slots = ((first_rows // quarter) ^ own_quarter) * (quarter // span) + first_rows % quarter // span
    late = 3
    early = chips - late
    parts = []
    for w in range(2):
        parts.append(project(slots, pieces[w], out_held[:early], late))

    out_columns = w_out.shape[1] // 2
    weight_own = lax.dynamic_slice_in_dim(value_weight, core * out_columns, out_columns, 0)
    pair_sums = jnp.stack(
        [
            finish(
                heads,
                out_held[early:],
                part,
                lax.dynamic_slice_in_dim(states, own_quarter * out_columns, out_columns, 1),
                weight_own[None, :],
            )[:2]
            for (part, heads), states in zip(parts, (hidden_in, states_got))
        ],
        1,
    )

    incoming, coming_old = suffix(known, place)
    advantage = local_part + bridge * coming_old + reach * incoming
    shared = swap(jnp.stack([advantage, old_values]))
    both_advantage = jnp.stack([advantage, shared[0]])
    both_old = jnp.stack([old_values, shared[1]])

    pair_sums = pair_sums + lax.ppermute(pair_sums, "mp", across)
    turned = swap(pair_sums)
    pair_sums = pair_sums.reshape(2, 2, rows) + turned.reshape(2, 2, rows)[:, ::-1]
    value = pair_sums[1] * lax.rsqrt(pair_sums[0] / width + epsilon)
    returns = both_advantage + both_old
    clipped = both_old + jnp.clip(value - both_old, -clip_range, clip_range)
    terms = jnp.maximum((value - returns) ** 2, (clipped - returns) ** 2)
    window_loss = jnp.sum(terms, 1)
    total_loss = window_loss[:1] + window_loss[1:]
    by = 2
    while by < devices:
        total_loss = total_loss + lax.ppermute(
            total_loss, "dp", [(i, i ^ by) for i in range(devices)]
        )
        by *= 2
    value_loss = 0.5 * total_loss[0] / (rows * devices)
    return (value[0], advantage, value_loss)


def suits(devices, sides, hidden, query, key):
    return (
        sides == 2
        and devices >= 16
        and devices & (devices - 1) == 0
        and key[1] == 4 * HEAD
        and query[1] * devices == 8 * hidden[1]
        and hidden[0] % 512 == 0
    )


def body(hidden_in, w_query, w_key, *rest):
    fits = suits(
        lax.axis_size("dp"), lax.axis_size("mp"), hidden_in.shape, w_query.shape, w_key.shape
    )
    return (shared_body if fits else plain_body)(hidden_in, w_query, w_key, *rest)


def solution(mesh):
    return jax.shard_map(
        body,
        mesh=mesh,
        in_specs=(
            P("dp", None),
            P("dp", "mp"),
            P("dp", "mp"),
            P("dp", "mp"),
            P("dp", "mp"),
            P("mp"),
            P("dp"),
            P("dp"),
            P(),
            P(),
        ),
        out_specs=(P("dp"), P("dp"), P()),
        check_vma=False,
    )
```

```python
import math

import jax
import jax.numpy as jnp
from jax import lax
from jax.experimental import pallas as pl
from jax.experimental.pallas import tpu as pltpu
from jax.sharding import PartitionSpec as P


HEAD = 128


discount = 0.999
trace_decay = 0.997
clip_range = 0.2
epsilon = 1e-05
rope_base = 500000.0


def from_behind(array, axis, by):
    size = lax.axis_size(axis)
    pairs = [(i, i + by) for i in range(size) if 0 <= i + by < size]
    return lax.ppermute(array, axis, pairs)


def carried_in(part, axis, combine, identity):
    count = lax.axis_size(axis)
    place = lax.axis_index(axis)
    ahead = count - 1 - place
    gathered = jax.tree.map(lambda a: lax.all_gather(a, axis), part)
    state = jax.tree.map(lambda a, e: jnp.zeros_like(a) + jnp.asarray(e, a.dtype), part, identity)

    def one(hop, state):
        source = count - 1 - hop
        return combine(
            state, jax.tree.map(lambda a: lax.dynamic_index_in_dim(a, source, 0, False), gathered)
        )

    return lax.fori_loop(0, ahead, one, state)


def rotate(states, positions):
    half = HEAD // 2
    freq = rope_base ** (-jnp.arange(half, dtype=jnp.float32) * 2.0 / HEAD)
    angles = positions[:, None] * freq[None, :]
    cosine = jnp.cos(angles)[:, None, :]
    sine = jnp.sin(angles)[:, None, :]
    first = states[..., :half]
    second = states[..., half:]
    return jnp.concatenate([first * cosine - second * sine, second * cosine + first * sine], -1)


def plain_body(
    hidden_in, w_query, w_key, w_value, w_out, value_weight, rewards, old_values, lengths, terminal
):
    rows = hidden_in.shape[0]
    width = hidden_in.shape[1]
    states = hidden_in.astype(jnp.float32)
    normed = (states * lax.rsqrt(jnp.mean(states * states, 1, keepdims=True) + epsilon)).astype(
        jnp.bfloat16
    )
    pieces = (
        lax.all_gather(w_query, "dp", axis=0, tiled=True),
        lax.all_gather(w_key, "dp", axis=0, tiled=True),
        lax.all_gather(w_value, "dp", axis=0, tiled=True),
        lax.all_gather(w_out, "dp", axis=0, tiled=True),
    )
    add_pieces = pieces[:3]
    summed = tuple(
        (jnp.dot(normed, piece, preferred_element_type=jnp.float32) for piece in add_pieces)
    )
    stored = pieces[3]
    query_sum, key_sum, value_sum, whole_out = summed + (stored,)
    position_ids = lax.axis_index("dp") * rows + jnp.arange(rows, dtype=jnp.int32)
    positions = position_ids.astype(jnp.float32)
    local_heads = w_query.shape[1] // HEAD
    local_kv = w_key.shape[1] // HEAD
    group = local_heads // local_kv
    query = rotate(query_sum.reshape(rows, local_heads, HEAD), positions).astype(jnp.bfloat16)
    key = rotate(key_sum.reshape(rows, local_kv, HEAD), positions).astype(jnp.bfloat16)
    values_proj = value_sum.astype(jnp.bfloat16).reshape(rows, local_kv, HEAD)
    ends = jnp.cumsum(lengths)
    matches = ends[None, :] - 1 == position_ids[:, None]
    finished = jnp.any(matches, 1).astype(jnp.float32)
    stopped = jnp.sum(jnp.where(matches, terminal[None, :], 0), 1).astype(jnp.float32)
    episode = jnp.sum((ends[None, :] <= position_ids[:, None]).astype(jnp.int32), 1)
    order = jnp.arange(rows, dtype=jnp.int32)
    same_episode = episode[None, :] == episode[:, None]
    allowed = (order[None, :] <= order[:, None]) & same_episode
    scores = jnp.einsum(
        "tkgd,skd->kgts",
        query.reshape(rows, local_kv, group, HEAD),
        key,
        preferred_element_type=jnp.float32,
    ) * (1.0 / HEAD**0.5)
    masked = jnp.where(allowed[None, None], scores, -1e30)
    largest = jnp.max(masked, -1, keepdims=True)
    expon = jnp.where(allowed[None, None], jnp.exp(masked - largest), 0.0)
    probs = (expon / jnp.sum(expon, -1, keepdims=True)).astype(jnp.bfloat16)
    output = jnp.einsum("kgts,skd->tkgd", probs, values_proj, preferred_element_type=jnp.float32)
    attended = output.astype(jnp.bfloat16).reshape(rows, local_heads * HEAD)
    all_heads = lax.all_gather(attended, "mp", axis=1, tiled=True)
    projected = jnp.dot(all_heads, whole_out, preferred_element_type=jnp.float32)
    feature_count = w_out.shape[1]
    own_states = lax.dynamic_slice_in_dim(
        states, lax.axis_index("mp") * feature_count, feature_count, 1
    )
    residual = own_states + projected
    square_sum, head_sum = lax.psum(
        (jnp.sum(residual * residual, 1), jnp.sum(residual * value_weight[None, :], 1)), "mp"
    )
    value = head_sum * lax.rsqrt(square_sum / width + epsilon)
    following = from_behind(old_values[:1], "dp", -1)
    next_old = jnp.concatenate([old_values[1:], following])
    booted = jnp.where(finished > 0, (1.0 - stopped) * old_values, next_old)
    delta = rewards + discount * booted - old_values
    keep_rate = discount * trace_decay
    spacing = (order[None, :] - order[:, None]).astype(jnp.float32)
    forward_mask = (spacing >= 0.0) & same_episode
    decay_matrix = jnp.where(
        forward_mask, jnp.power(jnp.float32(keep_rate), jnp.maximum(spacing, 0.0)), 0.0
    )
    local_part = jnp.dot(decay_matrix, delta, precision=lax.Precision.HIGHEST)
    remaining = (rows - order).astype(jnp.float32)
    reach = jnp.where(episode == episode[-1], jnp.power(jnp.float32(keep_rate), remaining), 0.0) * (
        1.0 - finished[-1]
    )

    def compose(earlier, later_map):
        return (later_map[0] + later_map[1] * earlier[0], later_map[1] * earlier[1])

    prefix = carried_in(
        (local_part[:1], reach[:1]),
        "dp",
        compose,
        (jnp.zeros((1,), jnp.float32), jnp.ones((1,), jnp.float32)),
    )
    incoming = prefix[0][0]
    advantage = local_part + reach * incoming
    returns = advantage + old_values
    clipped = old_values + jnp.clip(value - old_values, -clip_range, clip_range)
    terms = jnp.maximum((value - returns) ** 2, (clipped - returns) ** 2)
    total_loss = lax.psum(jnp.sum(terms), "dp")
    value_loss = 0.5 * total_loss / (rows * lax.axis_size("dp"))
    return (value, advantage, value_loss)


def ring_order(chips):
    return list(range(0, chips, 2)) + list(range(chips - 1, 0, -2))


def ring_pairs(chips):
    order = ring_order(chips)
    pairs = []
    for spot in range(chips):
        here, there = order[spot], order[(spot + 1) % chips]
        pairs.append((2 * here, 2 * there))
        pairs.append((2 * there + 1, 2 * here + 1))
    return pairs


def ring_sources(chips):
    order = ring_order(chips)
    spots = {chip: spot for spot, chip in enumerate(order)}
    forward = [[order[(spots[c] - k) % chips] for k in range(chips)] for c in range(chips)]
    back = [[order[(spots[c] + k) % chips] for k in range(chips)] for c in range(chips)]
    return jnp.array([forward, back], jnp.int32)


def norm_kernel(sources, states_ref, normed_ref):
    width = states_ref.shape[1]
    chips = sources.shape[0]
    span = width // chips
    states = states_ref[...].astype(jnp.float32)
    scale = lax.rsqrt(jnp.mean(states * states, 1, keepdims=True) + epsilon)
    for k in range(chips):
        start = pl.multiple_of(sources[k] * span, span)
        piece = states_ref[:, pl.ds(start, span)].astype(jnp.float32)
        normed_ref[:, k * span : (k + 1) * span] = (piece * scale).astype(jnp.bfloat16)


def norm_in_order(states, sources, window, into=None):
    rows, width = states.shape
    tile = min(128, rows)
    steps = rows // tile
    operands = [states]
    specs = [pl.BlockSpec((tile, width), lambda i, s: (i, 0))]
    kernel = norm_kernel
    if into is not None:
        operands.append(into)
        specs.append(pl.BlockSpec(memory_space=pl.ANY))
        kernel = lambda s, x, _, o: norm_kernel(s, x, o)
    return pl.pallas_call(
        kernel,
        grid_spec=pltpu.PrefetchScalarGridSpec(
            num_scalar_prefetch=1,
            grid=(steps,),
            in_specs=specs,
            out_specs=pl.BlockSpec((tile, width), lambda i, s: (window * steps + i, 0)),
        ),
        out_shape=jax.ShapeDtypeStruct((2 * rows, width), jnp.bfloat16),
        input_output_aliases={} if into is None else {2: 0},
        cost_estimate=pl.CostEstimate(
            flops=4 * rows * width, bytes_accessed=4 * rows * width, transcendentals=rows
        ),
        compiler_params=pltpu.CompilerParams(vmem_limit_bytes=12 * 2**20),
    )(sources, *operands)


def spin(states, cosine, sine):
    return states * cosine + pltpu.roll(states, HEAD // 2, 1) * sine


def attend_kernel(query_ref, key_ref, val_ref, cos_ref, sin_ref, ep_col_ref, ep_row_ref, out_ref):
    rows = key_ref.shape[0]
    tile = rows // 2
    cosine = cos_ref[...]
    sine = sin_ref[...]
    key = spin(key_ref[...], cosine, sine).astype(jnp.bfloat16)
    vals = val_ref[...].astype(jnp.bfloat16)
    for t in range(2):
        low, high = t * tile, (t + 1) * tile
        at_row = lax.broadcasted_iota(jnp.int32, (tile, high), 0) + low
        at_col = lax.broadcasted_iota(jnp.int32, (tile, high), 1)
        allowed = (at_col <= at_row) & (ep_col_ref[low:high] == ep_row_ref[:, :high])
        bias = jnp.where(allowed, 0.0, -1e30)

        def some(step, _):
            for h in range(2):
                cut = pl.ds(pl.multiple_of((2 * step + h) * HEAD, HEAD), HEAD)
                query = spin(query_ref[low:high, cut], cosine[low:high], sine[low:high])
                scores = lax.dot_general(
                    query.astype(jnp.bfloat16),
                    key[:high],
                    (((1,), (1,)), ((), ())),
                    preferred_element_type=jnp.float32,
                )
                masked = scores * (1.0 / HEAD**0.5) + bias
                largest = jnp.max(masked, -1, keepdims=True)
                expon = jnp.exp(masked - largest)
                share = 1.0 / jnp.sum(expon, -1, keepdims=True)
                probs = (expon * share).astype(jnp.bfloat16)
                out_ref[low:high, cut] = jnp.dot(
                    probs, vals[:high], preferred_element_type=jnp.float32
                ).astype(jnp.bfloat16)
            return 0

        lax.fori_loop(0, query_ref.shape[1] // HEAD // 2, some, 0)


def attend(window, which, rows, query, kv, cosine, sine, ep_col, ep_row):
    kv_count = kv.shape[1] // HEAD // 2
    width = query.shape[1]
    heads = width // HEAD
    once = lambda i: (window, 0)
    return pl.pallas_call(
        attend_kernel,
        grid=(1,),
        in_specs=[
            pl.BlockSpec((rows, width), once),
            pl.BlockSpec((rows, HEAD), lambda i: (window, which)),
            pl.BlockSpec((rows, HEAD), lambda i: (window, kv_count + which)),
            pl.BlockSpec((rows, HEAD), once),
            pl.BlockSpec((rows, HEAD), once),
            pl.BlockSpec((rows, 1), once),
            pl.BlockSpec((1, rows), lambda i: (0, window)),
        ],
        out_specs=pl.BlockSpec((rows, width), lambda i: (0, 0)),
        out_shape=jax.ShapeDtypeStruct((rows, width), jnp.bfloat16),
        cost_estimate=pl.CostEstimate(
            flops=4 * heads * HEAD * rows * rows,
            bytes_accessed=6 * rows * width,
            transcendentals=heads * rows * rows,
        ),
        compiler_params=pltpu.CompilerParams(vmem_limit_bytes=12 * 2**20),
    )(query, kv, kv, cosine, sine, ep_col, ep_row)


def project_kernel(pieces, count, late, *refs):
    offsets = refs[0]
    piece_refs = refs[1 : 1 + pieces]
    weight_refs = refs[1 + pieces : 1 + pieces + 2 * count]
    total_ref, late_ref, heads_ref, weights, sems = refs[1 + pieces + 2 * count :]
    rows = piece_refs[0].shape[0]
    half = weights.shape[2]
    copies = [(ref, heads_ref.at[p]) for p, ref in enumerate(piece_refs)]
    copies += [(ref, weights.at[i]) for i, ref in enumerate(weight_refs)]
    copies = [pltpu.make_async_copy(*c, sems.at[i]) for i, c in enumerate(copies)]
    for copy in copies:
        copy.start()
    for copy in copies[:pieces]:
        copy.wait()
    for k in range(late):
        late_ref[k] = heads_ref[offsets[count + k]]
    tile = 256
    for k in range(count):
        copies[pieces + 2 * k].wait()
        copies[pieces + 2 * k + 1].wait()

    def one(step, _):
        at = pl.ds(pl.multiple_of(step * tile, tile), tile)
        for side in range(2):
            total = None
            for k in range(count):
                term = jnp.dot(
                    heads_ref[offsets[k], at],
                    weights[2 * k + side],
                    preferred_element_type=jnp.float32,
                )
                total = term if total is None else total + term
            total_ref[at, side * half : (side + 1) * half] = total
        return 0

    lax.fori_loop(0, rows // tile, one, 0)


def project(offsets, pieces, pairs, late):
    weights = [w for pair in pairs for w in pair]
    rows, span = pieces[0].shape
    half = weights[0].shape[1]
    number = len(pieces)
    count = len(pairs)
    here = pl.BlockSpec(memory_space=pltpu.HBM)
    vmem = pl.BlockSpec(memory_space=pltpu.VMEM)
    return pl.pallas_call(
        lambda *refs: project_kernel(number, count, late, *refs),
        in_specs=[pl.BlockSpec(memory_space=pltpu.SMEM)] + [here] * (number + len(weights)),
        out_specs=[vmem, vmem],
        out_shape=[
            jax.ShapeDtypeStruct((rows, 2 * half), jnp.float32),
            jax.ShapeDtypeStruct((late, rows, span), jnp.bfloat16),
        ],
        scratch_shapes=[
            pltpu.VMEM((number, rows, span), jnp.bfloat16),
            pltpu.VMEM((len(weights), span, half), jnp.bfloat16),
            pltpu.SemaphoreType.DMA((number + len(weights),)),
        ],
        compiler_params=pltpu.CompilerParams(vmem_limit_bytes=20 * 2**20),
        cost_estimate=pl.CostEstimate(
            flops=4 * rows * half * span * count,
            bytes_accessed=2 * rows * span * number + 8 * rows * half,
            transcendentals=0,
        ),
        name="project",
    )(offsets, *pieces, *weights)


def finish_kernel(late, heads_ref, *refs):
    weights = refs[: 2 * late]
    base_ref, states_ref, weight_ref, out_ref = refs[2 * late :]
    half = weights[0].shape[1]
    squares = headed = 0.0
    for side in range(2):
        cut = slice(side * half, (side + 1) * half)
        total = base_ref[:, cut]
        for k in range(late):
            total = total + jnp.dot(
                heads_ref[k], weights[2 * k + side][...], preferred_element_type=jnp.float32
            )
        residual = total + states_ref[:, cut].astype(jnp.float32)
        squares = squares + jnp.sum(residual * residual, 1, keepdims=True)
        headed = headed + jnp.sum(residual * weight_ref[:, cut], 1, keepdims=True)
    lane = lax.broadcasted_iota(jnp.int32, (squares.shape[0], HEAD), 1)
    out_ref[...] = jnp.where(lane == 0, squares, headed).T[: out_ref.shape[0]]


def finish(heads, pairs, base, states, weight):
    late, rows, span = heads.shape
    columns = base.shape[1]
    weights = [w for pair in pairs for w in pair]
    tile = 256
    whole = lambda i: (0, 0)
    return pl.pallas_call(
        lambda *refs: finish_kernel(late, *refs),
        grid=(rows // tile,),
        in_specs=[pl.BlockSpec((late, tile, span), lambda i: (0, i, 0))]
        + [pl.BlockSpec(w.shape, whole) for w in weights]
        + [
            pl.BlockSpec((tile, columns), lambda i: (i, 0)),
            pl.BlockSpec((tile, columns), lambda i: (i, 0)),
            pl.BlockSpec((1, columns), whole),
        ],
        out_specs=pl.BlockSpec((8, tile), lambda i: (0, i)),
        out_shape=jax.ShapeDtypeStruct((8, rows), jnp.float32),
        compiler_params=pltpu.CompilerParams(vmem_limit_bytes=16 * 2**20),
        cost_estimate=pl.CostEstimate(
            flops=2 * rows * columns * span * late,
            bytes_accessed=rows * (2 * late * span + 6 * columns),
            transcendentals=0,
        ),
        name="finish",
    )(heads, *weights, base, states, weight)


def tie(array, *others):
    return lax.optimization_barrier((array,) + others)[0]


def suffix_kernel(place_ref, maps_ref, out_ref):
    devices = maps_ref.shape[0]
    place = place_ref[0]
    total, old = jnp.float32(0.0), jnp.float32(0.0)
    for i in range(devices - 1, 0, -1):
        later = i > place
        fresh = maps_ref[i, 0] + maps_ref[i, 1] * old + maps_ref[i, 2] * total
        total = jnp.where(later, fresh, total)
        old = jnp.where(later, maps_ref[i, 3], old)
    out_ref[0] = total
    out_ref[1] = old


def suffix(maps, place):
    smem = pl.BlockSpec(memory_space=pltpu.SMEM)
    out = pl.pallas_call(
        suffix_kernel,
        in_specs=[smem, smem],
        out_specs=smem,
        out_shape=jax.ShapeDtypeStruct((2,), jnp.float32),
        compiler_params=pltpu.CompilerParams(vmem_limit_bytes=2**20),
        name="suffix",
    )(place.astype(jnp.int32).reshape(1), maps)
    return out[0], out[1]


def tie(array, *others):
    return lax.optimization_barrier((array,) + others)[0]


def shared_body(
    hidden_in, w_query, w_key, w_value, w_out, value_weight, rewards, old_values, lengths, terminal
):
    rows, width = hidden_in.shape
    devices = lax.axis_size("dp")
    place = lax.axis_index("dp")
    side = lax.axis_index("mp")
    core = place % 2
    chip = place // 2
    chips = devices // 2
    partner = [(i, i ^ 1) for i in range(devices)]
    across = [(0, 1), (1, 0)]
    ring = ring_pairs(chips)

    def swap(array):
        return lax.ppermute(array, "dp", partner)

    def pair_up(mine, got):
        return jnp.where(
            core == 0, jnp.concatenate([mine, got], 0), jnp.concatenate([got, mine], 0)
        )

    def columns(weight, which, part, parts):
        half = weight.shape[1] // 2
        size = half // parts
        return lax.dynamic_slice_in_dim(weight, which * half + part * size, size, 1)

    def chip_block(pieces):
        mine = jnp.concatenate([columns(w, core, *p) for w, *p in pieces], 1)
        theirs = jnp.concatenate([columns(w, 1 - core, *p) for w, *p in pieces], 1)
        return pair_up(mine, swap(theirs))

    local_kv = w_key.shape[1] // HEAD // 2
    group = w_query.shape[1] // w_key.shape[1]

    def hop(block):
        return lax.ppermute(block, "dp", ring)

    lanes = [chip_block([(w_key, 0, 1), (w_value, 0, 1)])]
    lanes += [chip_block([(w_query, j, local_kv)]) for j in range(local_kv)]
    first_hops = [hop(block) for block in lanes]
    states_got = swap(hidden_in)
    sources = ring_sources(chips)[core, chip]
    place, lengths, rewards, old_values, *_ = lax.optimization_barrier(
        (place, lengths, rewards, old_values, *lanes)
    )
    span = width // chips

    ends = jnp.cumsum(lengths)
    order = jnp.arange(rows, dtype=jnp.int32)
    position_ids = place * rows + order
    other_ids = (place + 1 - 2 * core) * rows + order
    both_ids = jnp.concatenate([position_ids, other_ids])
    half = HEAD // 2
    freq = rope_base ** (-jnp.arange(half, dtype=jnp.float32) * 2.0 / HEAD)
    angles = both_ids.astype(jnp.float32)[:, None] * freq[None, :]
    cosine = jnp.cos(angles)
    sine = jnp.sin(angles)
    cosine = jnp.concatenate([cosine, cosine], 1)
    sine = jnp.concatenate([-sine, sine], 1)
    both_episode = jnp.sum((ends[None, :] <= both_ids[:, None]).astype(jnp.int32), 1)

    matches = ends[None, :] - 1 == position_ids[:, None]
    finished = jnp.any(matches, 1).astype(jnp.float32)
    stopped = jnp.sum(jnp.where(matches, terminal[None, :], 0), 1).astype(jnp.float32)
    episode = both_episode[:rows]
    same_episode = episode[None, :] == episode[:, None]
    next_known = jnp.concatenate([old_values[1:], jnp.zeros((1,), jnp.float32)])
    booted = jnp.where(finished > 0, (1.0 - stopped) * old_values, next_known)
    delta = rewards + discount * booted - old_values
    keep_rate = discount * trace_decay

    def powers(number):
        return jnp.exp(number * math.log(keep_rate))

    spacing = (order[None, :] - order[:, None]).astype(jnp.float32)
    forward_mask = (spacing >= 0.0) & same_episode
    decay_matrix = jnp.where(
        forward_mask, powers(jnp.maximum(spacing, 0.0)), 0.0
    )
    local_part = jnp.dot(decay_matrix, delta, precision=lax.Precision.HIGHEST)
    remaining = (rows - order).astype(jnp.float32)
    open_end = 1.0 - finished[-1]
    reach = jnp.where(episode == episode[-1], powers(remaining), 0.0) * open_end
    bridge = reach / trace_decay
    maps = jnp.stack([local_part[0], bridge[0], reach[0], old_values[0]])
    known = jnp.where(jnp.arange(devices)[:, None] == place, maps[None, :], 0.0)

    normed = norm_in_order(hidden_in, sources, 0)
    normed = norm_in_order(states_got, sources, 1, normed)

    def use(total, k, block):
        term = jnp.dot(
            normed[:, k * span : (k + 1) * span], block, preferred_element_type=jnp.float32
        )
        return term if total is None else total + term

    sums = [use(None, 0, block) for block in lanes]
    blocks = first_hops
    for k in range(1, chips):
        if k + 1 < chips:
            coming = [hop(block) for block in blocks]
        sums = [use(sums[lane], k, block) for lane, block in enumerate(blocks)]
        step = 2 ** (k - 1)
        if step < devices:
            moved = lax.ppermute(
                tie(known, blocks[0]), "dp", [(i, i ^ step) for i in range(devices)]
            )
            known = known + moved
        if k == chips - 3:
            out_blocks = [chip_block([(tie(w_out, blocks[0]), j, 2)]) for j in range(2)]
        if 3 <= k < chips - 1:
            sums = [tie(total, blocks[0]) for total in sums]
        last_blocks = blocks
        blocks = coming
    out_held = [out_blocks]
    for k in range(1, chips):
        out_held.append(
            [
                hop(tie(block, last_blocks[j]) if k == 1 else block)
                for j, block in enumerate(out_held[-1])
            ]
        )

    pieces = [[], []]
    sent = {}
    for w in range(2):
        for j in range(local_kv):
            part = attend(
                w, j, rows, sums[1 + j], sums[0], cosine, sine,
                both_episode[:, None], both_episode[None, :],
            )
            sent[w, j] = (part, lax.ppermute(part, "mp", across))
    diagonal = {}
    for n, (w, j) in enumerate((w, j) for w in range(2) for j in range(local_kv)):
        after = out_held[min(n + 2, chips - 2)]
        diagonal[1 - w, j] = swap(tie(sent[w, j][1], *after))
    for w in range(2):
        pieces[w] = [sent[w, j][0] for j in range(local_kv)]
        pieces[w] += [swap(sent[1 - w, j][0]) for j in range(local_kv)]
        pieces[w] += [sent[w, j][1] for j in range(local_kv)]
        pieces[w] += [diagonal[w, j] for j in range(local_kv)]

    quarter = local_kv * group * HEAD
    own_quarter = side * 2 + core
    first_rows = sources * span
    slots = ((first_rows // quarter) ^ own_quarter) * (quarter // span) + first_rows % quarter // span
    late = 3
    early = chips - late
    parts = []
    for w in range(2):
        parts.append(project(slots, pieces[w], out_held[:early], late))

    out_columns = w_out.shape[1] // 2
    weight_own = lax.dynamic_slice_in_dim(value_weight, core * out_columns, out_columns, 0)
    pair_sums = jnp.stack(
        [
            finish(
                heads,
                out_held[early:],
                part,
                lax.dynamic_slice_in_dim(states, own_quarter * out_columns, out_columns, 1),
                weight_own[None, :],
            )[:2]
            for (part, heads), states in zip(parts, (hidden_in, states_got))
        ],
        1,
    )

    incoming, coming_old = suffix(known, place)
    advantage = local_part + bridge * coming_old + reach * incoming
    shared = swap(jnp.stack([advantage, old_values]))
    both_advantage = jnp.stack([advantage, shared[0]])
    both_old = jnp.stack([old_values, shared[1]])

    pair_sums = pair_sums + lax.ppermute(pair_sums, "mp", across)
    turned = swap(pair_sums)
    pair_sums = pair_sums.reshape(2, 2, rows) + turned.reshape(2, 2, rows)[:, ::-1]
    value = pair_sums[1] * lax.rsqrt(pair_sums[0] / width + epsilon)
    returns = both_advantage + both_old
    clipped = both_old + jnp.clip(value - both_old, -clip_range, clip_range)
    terms = jnp.maximum((value - returns) ** 2, (clipped - returns) ** 2)
    window_loss = jnp.sum(terms, 1)
    total_loss = window_loss[:1] + window_loss[1:]
    by = 2
    while by < devices:
        total_loss = total_loss + lax.ppermute(
            total_loss, "dp", [(i, i ^ by) for i in range(devices)]
        )
        by *= 2
    value_loss = 0.5 * total_loss[0] / (rows * devices)
    return (value[0], advantage, value_loss)


def suits(devices, sides, hidden, query, key):
    return (
        sides == 2
        and devices >= 16
        and devices & (devices - 1) == 0
        and key[1] == 4 * HEAD
        and query[1] * devices == 8 * hidden[1]
        and hidden[0] % 512 == 0
    )


def body(hidden_in, w_query, w_key, *rest):
    fits = suits(
        lax.axis_size("dp"), lax.axis_size("mp"), hidden_in.shape, w_query.shape, w_key.shape
    )
    return (shared_body if fits else plain_body)(hidden_in, w_query, w_key, *rest)


def solution(mesh):
    return jax.shard_map(
        body,
        mesh=mesh,
        in_specs=(
            P("dp", None),
            P("dp", "mp"),
            P("dp", "mp"),
            P("dp", "mp"),
            P("dp", "mp"),
            P("mp"),
            P("dp"),
            P("dp"),
            P(),
            P(),
        ),
        out_specs=(P("dp"), P("dp"), P()),
        check_vma=False,
    )
```

```python
import math

import jax
import jax.numpy as jnp
from jax import lax
from jax.experimental import pallas as pl
from jax.experimental.pallas import tpu as pltpu
from jax.sharding import PartitionSpec as P


HEAD = 128


discount = 0.999
trace_decay = 0.997
clip_range = 0.2
epsilon = 1e-05
rope_base = 500000.0


def from_behind(array, axis, by):
    size = lax.axis_size(axis)
    pairs = [(i, i + by) for i in range(size) if 0 <= i + by < size]
    return lax.ppermute(array, axis, pairs)


def carried_in(part, axis, combine, identity):
    count = lax.axis_size(axis)
    place = lax.axis_index(axis)
    ahead = count - 1 - place
    gathered = jax.tree.map(lambda a: lax.all_gather(a, axis), part)
    state = jax.tree.map(lambda a, e: jnp.zeros_like(a) + jnp.asarray(e, a.dtype), part, identity)

    def one(hop, state):
        source = count - 1 - hop
        return combine(
            state, jax.tree.map(lambda a: lax.dynamic_index_in_dim(a, source, 0, False), gathered)
        )

    return lax.fori_loop(0, ahead, one, state)


def rotate(states, positions):
    half = HEAD // 2
    freq = rope_base ** (-jnp.arange(half, dtype=jnp.float32) * 2.0 / HEAD)
    angles = positions[:, None] * freq[None, :]
    cosine = jnp.cos(angles)[:, None, :]
    sine = jnp.sin(angles)[:, None, :]
    first = states[..., :half]
    second = states[..., half:]
    return jnp.concatenate([first * cosine - second * sine, second * cosine + first * sine], -1)


def plain_body(
    hidden_in, w_query, w_key, w_value, w_out, value_weight, rewards, old_values, lengths, terminal
):
    rows = hidden_in.shape[0]
    width = hidden_in.shape[1]
    states = hidden_in.astype(jnp.float32)
    normed = (states * lax.rsqrt(jnp.mean(states * states, 1, keepdims=True) + epsilon)).astype(
        jnp.bfloat16
    )
    pieces = (
        lax.all_gather(w_query, "dp", axis=0, tiled=True),
        lax.all_gather(w_key, "dp", axis=0, tiled=True),
        lax.all_gather(w_value, "dp", axis=0, tiled=True),
        lax.all_gather(w_out, "dp", axis=0, tiled=True),
    )
    add_pieces = pieces[:3]
    summed = tuple(
        (jnp.dot(normed, piece, preferred_element_type=jnp.float32) for piece in add_pieces)
    )
    stored = pieces[3]
    query_sum, key_sum, value_sum, whole_out = summed + (stored,)
    position_ids = lax.axis_index("dp") * rows + jnp.arange(rows, dtype=jnp.int32)
    positions = position_ids.astype(jnp.float32)
    local_heads = w_query.shape[1] // HEAD
    local_kv = w_key.shape[1] // HEAD
    group = local_heads // local_kv
    query = rotate(query_sum.reshape(rows, local_heads, HEAD), positions).astype(jnp.bfloat16)
    key = rotate(key_sum.reshape(rows, local_kv, HEAD), positions).astype(jnp.bfloat16)
    values_proj = value_sum.astype(jnp.bfloat16).reshape(rows, local_kv, HEAD)
    ends = jnp.cumsum(lengths)
    matches = ends[None, :] - 1 == position_ids[:, None]
    finished = jnp.any(matches, 1).astype(jnp.float32)
    stopped = jnp.sum(jnp.where(matches, terminal[None, :], 0), 1).astype(jnp.float32)
    episode = jnp.sum((ends[None, :] <= position_ids[:, None]).astype(jnp.int32), 1)
    order = jnp.arange(rows, dtype=jnp.int32)
    same_episode = episode[None, :] == episode[:, None]
    allowed = (order[None, :] <= order[:, None]) & same_episode
    scores = jnp.einsum(
        "tkgd,skd->kgts",
        query.reshape(rows, local_kv, group, HEAD),
        key,
        preferred_element_type=jnp.float32,
    ) * (1.0 / HEAD**0.5)
    masked = jnp.where(allowed[None, None], scores, -1e30)
    largest = jnp.max(masked, -1, keepdims=True)
    expon = jnp.where(allowed[None, None], jnp.exp(masked - largest), 0.0)
    probs = (expon / jnp.sum(expon, -1, keepdims=True)).astype(jnp.bfloat16)
    output = jnp.einsum("kgts,skd->tkgd", probs, values_proj, preferred_element_type=jnp.float32)
    attended = output.astype(jnp.bfloat16).reshape(rows, local_heads * HEAD)
    all_heads = lax.all_gather(attended, "mp", axis=1, tiled=True)
    projected = jnp.dot(all_heads, whole_out, preferred_element_type=jnp.float32)
    feature_count = w_out.shape[1]
    own_states = lax.dynamic_slice_in_dim(
        states, lax.axis_index("mp") * feature_count, feature_count, 1
    )
    residual = own_states + projected
    square_sum, head_sum = lax.psum(
        (jnp.sum(residual * residual, 1), jnp.sum(residual * value_weight[None, :], 1)), "mp"
    )
    value = head_sum * lax.rsqrt(square_sum / width + epsilon)
    following = from_behind(old_values[:1], "dp", -1)
    next_old = jnp.concatenate([old_values[1:], following])
    booted = jnp.where(finished > 0, (1.0 - stopped) * old_values, next_old)
    delta = rewards + discount * booted - old_values
    keep_rate = discount * trace_decay
    spacing = (order[None, :] - order[:, None]).astype(jnp.float32)
    forward_mask = (spacing >= 0.0) & same_episode
    decay_matrix = jnp.where(
        forward_mask, jnp.power(jnp.float32(keep_rate), jnp.maximum(spacing, 0.0)), 0.0
    )
    local_part = jnp.dot(decay_matrix, delta, precision=lax.Precision.HIGHEST)
    remaining = (rows - order).astype(jnp.float32)
    reach = jnp.where(episode == episode[-1], jnp.power(jnp.float32(keep_rate), remaining), 0.0) * (
        1.0 - finished[-1]
    )

    def compose(earlier, later_map):
        return (later_map[0] + later_map[1] * earlier[0], later_map[1] * earlier[1])

    prefix = carried_in(
        (local_part[:1], reach[:1]),
        "dp",
        compose,
        (jnp.zeros((1,), jnp.float32), jnp.ones((1,), jnp.float32)),
    )
    incoming = prefix[0][0]
    advantage = local_part + reach * incoming
    returns = advantage + old_values
    clipped = old_values + jnp.clip(value - old_values, -clip_range, clip_range)
    terms = jnp.maximum((value - returns) ** 2, (clipped - returns) ** 2)
    total_loss = lax.psum(jnp.sum(terms), "dp")
    value_loss = 0.5 * total_loss / (rows * lax.axis_size("dp"))
    return (value, advantage, value_loss)


def ring_order(chips):
    return list(range(0, chips, 2)) + list(range(chips - 1, 0, -2))


def ring_pairs(chips):
    order = ring_order(chips)
    pairs = []
    for spot in range(chips):
        here, there = order[spot], order[(spot + 1) % chips]
        pairs.append((2 * here, 2 * there))
        pairs.append((2 * there + 1, 2 * here + 1))
    return pairs


def ring_sources(chips):
    order = ring_order(chips)
    spots = {chip: spot for spot, chip in enumerate(order)}
    forward = [[order[(spots[c] - k) % chips] for k in range(chips)] for c in range(chips)]
    back = [[order[(spots[c] + k) % chips] for k in range(chips)] for c in range(chips)]
    return jnp.array([forward, back], jnp.int32)


def norm_kernel(sources, states_ref, normed_ref):
    width = states_ref.shape[1]
    chips = sources.shape[0]
    span = width // chips
    states = states_ref[...].astype(jnp.float32)
    scale = lax.rsqrt(jnp.mean(states * states, 1, keepdims=True) + epsilon)
    for k in range(chips):
        start = pl.multiple_of(sources[k] * span, span)
        piece = states_ref[:, pl.ds(start, span)].astype(jnp.float32)
        normed_ref[:, k * span : (k + 1) * span] = (piece * scale).astype(jnp.bfloat16)


def norm_in_order(states, sources, window, into=None):
    rows, width = states.shape
    tile = min(128, rows)
    steps = rows // tile
    operands = [states]
    specs = [pl.BlockSpec((tile, width), lambda i, s: (i, 0))]
    kernel = norm_kernel
    if into is not None:
        operands.append(into)
        specs.append(pl.BlockSpec(memory_space=pl.ANY))
        kernel = lambda s, x, _, o: norm_kernel(s, x, o)
    return pl.pallas_call(
        kernel,
        grid_spec=pltpu.PrefetchScalarGridSpec(
            num_scalar_prefetch=1,
            grid=(steps,),
            in_specs=specs,
            out_specs=pl.BlockSpec((tile, width), lambda i, s: (window * steps + i, 0)),
        ),
        out_shape=jax.ShapeDtypeStruct((2 * rows, width), jnp.bfloat16),
        input_output_aliases={} if into is None else {2: 0},
        cost_estimate=pl.CostEstimate(
            flops=4 * rows * width, bytes_accessed=4 * rows * width, transcendentals=rows
        ),
        compiler_params=pltpu.CompilerParams(vmem_limit_bytes=12 * 2**20),
    )(sources, *operands)


def spin(states, cosine, sine):
    return states * cosine + pltpu.roll(states, HEAD // 2, 1) * sine


def attend_kernel(window, query_ref, key_ref, val_ref, cos_ref, sin_ref, ep_col_ref, ep_row_ref, out_ref):
    rows = key_ref.shape[0]
    tile = rows // 2
    lane = lax.broadcasted_iota(jnp.int32, cos_ref.shape, 1)
    lower = lane < HEAD // 2

    def widen(table):
        turned = pltpu.roll(table, HEAD // 2, 1)
        return jnp.where(lower, table, turned) if window == 0 else jnp.where(lower, turned, table)

    cosine = widen(cos_ref[...])
    sine = widen(sin_ref[...])
    sine = jnp.where(lower, -sine, sine)
    key = spin(key_ref[...], cosine, sine).astype(jnp.bfloat16)
    vals = val_ref[...].astype(jnp.bfloat16)
    for t in range(2):
        low, high = t * tile, (t + 1) * tile
        at_row = lax.broadcasted_iota(jnp.int32, (tile, high), 0) + low
        at_col = lax.broadcasted_iota(jnp.int32, (tile, high), 1)
        allowed = (at_col <= at_row) & (ep_col_ref[low:high] == ep_row_ref[:, :high])
        bias = jnp.where(allowed, 0.0, -1e30)

        def some(step, _):
            for h in range(2):
                cut = pl.ds(pl.multiple_of((2 * step + h) * HEAD, HEAD), HEAD)
                query = spin(query_ref[low:high, cut], cosine[low:high], sine[low:high])
                scores = lax.dot_general(
                    query.astype(jnp.bfloat16),
                    key[:high],
                    (((1,), (1,)), ((), ())),
                    preferred_element_type=jnp.float32,
                )
                masked = scores * (1.0 / HEAD**0.5) + bias
                largest = jnp.max(masked, -1, keepdims=True)
                expon = jnp.exp(masked - largest)
                share = 1.0 / jnp.sum(expon, -1, keepdims=True)
                probs = (expon * share).astype(jnp.bfloat16)
                out_ref[low:high, cut] = jnp.dot(
                    probs, vals[:high], preferred_element_type=jnp.float32
                ).astype(jnp.bfloat16)
            return 0

        lax.fori_loop(0, query_ref.shape[1] // HEAD // 2, some, 0)


def attend(window, which, rows, query, kv, cosine, sine, ep_col, ep_row):
    kv_count = kv.shape[1] // HEAD // 2
    width = query.shape[1]
    heads = width // HEAD
    once = lambda i: (window, 0)
    return pl.pallas_call(
        lambda *refs: attend_kernel(window, *refs),
        grid=(1,),
        in_specs=[
            pl.BlockSpec((rows, width), once),
            pl.BlockSpec((rows, HEAD), lambda i: (window, which)),
            pl.BlockSpec((rows, HEAD), lambda i: (window, kv_count + which)),
            pl.BlockSpec((rows, HEAD), lambda i: (0, 0)),
            pl.BlockSpec((rows, HEAD), lambda i: (0, 0)),
            pl.BlockSpec((rows, 1), once),
            pl.BlockSpec((1, rows), lambda i: (0, window)),
        ],
        out_specs=pl.BlockSpec((rows, width), lambda i: (0, 0)),
        out_shape=jax.ShapeDtypeStruct((rows, width), jnp.bfloat16),
        cost_estimate=pl.CostEstimate(
            flops=4 * heads * HEAD * rows * rows,
            bytes_accessed=6 * rows * width,
            transcendentals=heads * rows * rows,
        ),
        compiler_params=pltpu.CompilerParams(vmem_limit_bytes=12 * 2**20),
    )(query, kv, kv, cosine, sine, ep_col, ep_row)


def project_kernel(pieces, count, late, *refs):
    offsets = refs[0]
    piece_refs = refs[1 : 1 + pieces]
    weight_refs = refs[1 + pieces : 1 + pieces + 2 * count]
    total_ref, late_ref, heads_ref, weights, sems = refs[1 + pieces + 2 * count :]
    rows = piece_refs[0].shape[0]
    half = weights.shape[2]
    copies = [(ref, heads_ref.at[p]) for p, ref in enumerate(piece_refs)]
    copies += [(ref, weights.at[i]) for i, ref in enumerate(weight_refs)]
    copies = [pltpu.make_async_copy(*c, sems.at[i]) for i, c in enumerate(copies)]
    for copy in copies:
        copy.start()
    for copy in copies[:pieces]:
        copy.wait()
    for k in range(late):
        late_ref[k] = heads_ref[offsets[count + k]]
    tile = 256
    for k in range(count):
        copies[pieces + 2 * k].wait()
        copies[pieces + 2 * k + 1].wait()

    def one(step, _):
        at = pl.ds(pl.multiple_of(step * tile, tile), tile)
        for side in range(2):
            total = None
            for k in range(count):
                term = jnp.dot(
                    heads_ref[offsets[k], at],
                    weights[2 * k + side],
                    preferred_element_type=jnp.float32,
                )
                total = term if total is None else total + term
            total_ref[at, side * half : (side + 1) * half] = total
        return 0

    lax.fori_loop(0, rows // tile, one, 0)


def project(offsets, pieces, pairs, late):
    weights = [w for pair in pairs for w in pair]
    rows, span = pieces[0].shape
    half = weights[0].shape[1]
    number = len(pieces)
    count = len(pairs)
    here = pl.BlockSpec(memory_space=pltpu.HBM)
    vmem = pl.BlockSpec(memory_space=pltpu.VMEM)
    return pl.pallas_call(
        lambda *refs: project_kernel(number, count, late, *refs),
        in_specs=[pl.BlockSpec(memory_space=pltpu.SMEM)] + [here] * (number + len(weights)),
        out_specs=[vmem, vmem],
        out_shape=[
            jax.ShapeDtypeStruct((rows, 2 * half), jnp.float32),
            jax.ShapeDtypeStruct((late, rows, span), jnp.bfloat16),
        ],
        scratch_shapes=[
            pltpu.VMEM((number, rows, span), jnp.bfloat16),
            pltpu.VMEM((len(weights), span, half), jnp.bfloat16),
            pltpu.SemaphoreType.DMA((number + len(weights),)),
        ],
        compiler_params=pltpu.CompilerParams(vmem_limit_bytes=20 * 2**20),
        cost_estimate=pl.CostEstimate(
            flops=4 * rows * half * span * count,
            bytes_accessed=2 * rows * span * number + 8 * rows * half,
            transcendentals=0,
        ),
        name="project",
    )(offsets, *pieces, *weights)


def finish_kernel(late, heads_ref, *refs):
    weights = refs[: 2 * late]
    base_ref, states_ref, weight_ref, out_ref = refs[2 * late :]
    half = weights[0].shape[1]
    squares = headed = 0.0
    for side in range(2):
        cut = slice(side * half, (side + 1) * half)
        total = base_ref[:, cut]
        for k in range(late):
            total = total + jnp.dot(
                heads_ref[k], weights[2 * k + side][...], preferred_element_type=jnp.float32
            )
        residual = total + states_ref[:, cut].astype(jnp.float32)
        squares = squares + jnp.sum(residual * residual, 1, keepdims=True)
        headed = headed + jnp.sum(residual * weight_ref[:, cut], 1, keepdims=True)
    lane = lax.broadcasted_iota(jnp.int32, (squares.shape[0], HEAD), 1)
    out_ref[...] = jnp.where(lane == 0, squares, headed).T[: out_ref.shape[0]]


def finish(heads, pairs, base, states, weight):
    late, rows, span = heads.shape
    columns = base.shape[1]
    weights = [w for pair in pairs for w in pair]
    tile = 256
    whole = lambda i: (0, 0)
    return pl.pallas_call(
        lambda *refs: finish_kernel(late, *refs),
        grid=(rows // tile,),
        in_specs=[pl.BlockSpec((late, tile, span), lambda i: (0, i, 0))]
        + [pl.BlockSpec(w.shape, whole) for w in weights]
        + [
            pl.BlockSpec((tile, columns), lambda i: (i, 0)),
            pl.BlockSpec((tile, columns), lambda i: (i, 0)),
            pl.BlockSpec((1, columns), whole),
        ],
        out_specs=pl.BlockSpec((8, tile), lambda i: (0, i)),
        out_shape=jax.ShapeDtypeStruct((8, rows), jnp.float32),
        compiler_params=pltpu.CompilerParams(vmem_limit_bytes=16 * 2**20),
        cost_estimate=pl.CostEstimate(
            flops=2 * rows * columns * span * late,
            bytes_accessed=rows * (2 * late * span + 6 * columns),
            transcendentals=0,
        ),
        name="finish",
    )(heads, *weights, base, states, weight)


def tie(array, *others):
    return lax.optimization_barrier((array,) + others)[0]


def suffix_kernel(place_ref, maps_ref, out_ref):
    devices = maps_ref.shape[0]
    place = place_ref[0]
    total, old = jnp.float32(0.0), jnp.float32(0.0)
    for i in range(devices - 1, 0, -1):
        later = i > place
        fresh = maps_ref[i, 0] + maps_ref[i, 1] * old + maps_ref[i, 2] * total
        total = jnp.where(later, fresh, total)
        old = jnp.where(later, maps_ref[i, 3], old)
    out_ref[0] = total
    out_ref[1] = old


def suffix(maps, place):
    smem = pl.BlockSpec(memory_space=pltpu.SMEM)
    out = pl.pallas_call(
        suffix_kernel,
        in_specs=[smem, smem],
        out_specs=smem,
        out_shape=jax.ShapeDtypeStruct((2,), jnp.float32),
        compiler_params=pltpu.CompilerParams(vmem_limit_bytes=2**20),
        name="suffix",
    )(place.astype(jnp.int32).reshape(1), maps)
    return out[0], out[1]


def tie(array, *others):
    return lax.optimization_barrier((array,) + others)[0]


def shared_body(
    hidden_in, w_query, w_key, w_value, w_out, value_weight, rewards, old_values, lengths, terminal
):
    rows, width = hidden_in.shape
    devices = lax.axis_size("dp")
    place = lax.axis_index("dp")
    side = lax.axis_index("mp")
    core = place % 2
    chip = place // 2
    chips = devices // 2
    partner = [(i, i ^ 1) for i in range(devices)]
    across = [(0, 1), (1, 0)]
    ring = ring_pairs(chips)

    def swap(array):
        return lax.ppermute(array, "dp", partner)

    def pair_up(mine, got):
        return jnp.where(
            core == 0, jnp.concatenate([mine, got], 0), jnp.concatenate([got, mine], 0)
        )

    def columns(weight, which, part, parts):
        half = weight.shape[1] // 2
        size = half // parts
        return lax.dynamic_slice_in_dim(weight, which * half + part * size, size, 1)

    def chip_block(pieces):
        mine = jnp.concatenate([columns(w, core, *p) for w, *p in pieces], 1)
        theirs = jnp.concatenate([columns(w, 1 - core, *p) for w, *p in pieces], 1)
        return pair_up(mine, swap(theirs))

    local_kv = w_key.shape[1] // HEAD // 2
    group = w_query.shape[1] // w_key.shape[1]

    def hop(block):
        return lax.ppermute(block, "dp", ring)

    lanes = [chip_block([(w_key, 0, 1), (w_value, 0, 1)])]
    lanes += [chip_block([(w_query, j, local_kv)]) for j in range(local_kv)]
    first_hops = [hop(block) for block in lanes]
    states_got = swap(hidden_in)
    sources = ring_sources(chips)[core, chip]
    span = width // chips

    def marks(place, lengths):
        ends = jnp.cumsum(lengths)
        order = jnp.arange(rows, dtype=jnp.int32)
        position_ids = place * rows + order
        other_ids = (place + 1 - 2 * core) * rows + order
        both_ids = jnp.concatenate([position_ids, other_ids])
        half = HEAD // 2
        lane = jnp.arange(HEAD, dtype=jnp.int32)
        freq = rope_base ** (-(lane % half).astype(jnp.float32) * 2.0 / HEAD)
        spot = jnp.where(lane[None, :] < half, position_ids[:, None], other_ids[:, None])
        angles = spot.astype(jnp.float32) * freq[None, :]
        cosine = jnp.cos(angles)
        sine = jnp.sin(angles)
        both_episode = jnp.sum((ends[None, :] <= both_ids[:, None]).astype(jnp.int32), 1)
        return cosine, sine, both_episode, ends, position_ids, order

    def steps(place, marked, terminal, rewards, old_values):
        both_episode, ends, position_ids, order = marked
        matches = ends[None, :] - 1 == position_ids[:, None]
        finished = jnp.any(matches, 1).astype(jnp.float32)
        stopped = jnp.sum(jnp.where(matches, terminal[None, :], 0), 1).astype(jnp.float32)
        episode = both_episode[:rows]
        same_episode = episode[None, :] == episode[:, None]
        next_known = jnp.concatenate([old_values[1:], jnp.zeros((1,), jnp.float32)])
        booted = jnp.where(finished > 0, (1.0 - stopped) * old_values, next_known)
        delta = rewards + discount * booted - old_values
        keep_rate = discount * trace_decay

        def powers(number):
            return jnp.exp(number * math.log(keep_rate))

        spacing = (order[None, :] - order[:, None]).astype(jnp.float32)
        forward_mask = (spacing >= 0.0) & same_episode
        decay_matrix = jnp.where(
            forward_mask, powers(jnp.maximum(spacing, 0.0)), 0.0
        )
        local_part = jnp.dot(decay_matrix, delta, precision=lax.Precision.HIGHEST)
        remaining = (rows - order).astype(jnp.float32)
        open_end = 1.0 - finished[-1]
        reach = jnp.where(episode == episode[-1], powers(remaining), 0.0) * open_end
        bridge = reach / trace_decay
        row = lax.broadcasted_iota(jnp.int32, (devices, 4), 0)
        column = lax.broadcasted_iota(jnp.int32, (devices, 4), 1)
        known = jnp.where(column == 0, local_part[0], old_values[0])
        known = jnp.where(column == 1, bridge[0], jnp.where(column == 2, reach[0], known))
        known = jnp.where(row == place, known, 0.0)
        return local_part, bridge, reach, known

    normed = norm_in_order(hidden_in, sources, 0)
    normed = norm_in_order(states_got, sources, 1, normed)

    def use(total, k, block):
        term = jnp.dot(
            normed[:, k * span : (k + 1) * span], block, preferred_element_type=jnp.float32
        )
        return term if total is None else total + term

    sums = [use(None, 0, block) for block in lanes]
    blocks = first_hops
    for k in range(1, chips):
        if k + 1 < chips:
            coming = [hop(block) for block in blocks]
        sums = [use(sums[lane], k, block) for lane, block in enumerate(blocks)]
        if k == 4:
            *later, _ = lax.optimization_barrier((place, lengths, sums[0]))
            cosine, sine, *marked = marks(*later)
            both_episode = marked[0]
        if k == 5:
            *later, _ = lax.optimization_barrier(
                (place, tuple(marked), terminal, rewards, old_values, sums[0])
            )
            local_part, bridge, reach, known = steps(*later)
        step = 2 ** max(k - 6, 0)
        if k > 5:
            moved = lax.ppermute(
                tie(known, blocks[0]), "dp", [(i, i ^ step) for i in range(devices)]
            )
            known = known + moved
        if k == chips - 3:
            out_blocks = [chip_block([(tie(w_out, blocks[0]), j, 2)]) for j in range(2)]
        if 3 <= k < chips - 1:
            sums = [tie(total, blocks[0]) for total in sums]
        last_blocks = blocks
        blocks = coming
    out_held = [out_blocks]
    for k in range(1, chips):
        out_held.append(
            [
                hop(tie(block, last_blocks[j]) if k == 1 else block)
                for j, block in enumerate(out_held[-1])
            ]
        )

    number = chips - 6
    while 2**number < devices:
        step = 2**number
        moved = lax.ppermute(
            tie(known, out_held[2 * number - 2][0]), "dp", [(i, i ^ step) for i in range(devices)]
        )
        known = known + moved
        number += 1
    pieces = [[], []]
    sent = {}
    for w in range(2):
        for j in range(local_kv):
            part = attend(
                w, j, rows, sums[1 + j], sums[0], cosine, sine,
                both_episode[:, None], both_episode[None, :],
            )
            sent[w, j] = (part, lax.ppermute(part, "mp", across))
    diagonal = {}
    for n, (w, j) in enumerate((w, j) for w in range(2) for j in range(local_kv)):
        after = out_held[min(n + 2, chips - 2)]
        diagonal[1 - w, j] = swap(tie(sent[w, j][1], *after))
    for w in range(2):
        pieces[w] = [sent[w, j][0] for j in range(local_kv)]
        pieces[w] += [swap(sent[1 - w, j][0]) for j in range(local_kv)]
        pieces[w] += [sent[w, j][1] for j in range(local_kv)]
        pieces[w] += [diagonal[w, j] for j in range(local_kv)]

    quarter = local_kv * group * HEAD
    own_quarter = side * 2 + core
    first_rows = sources * span
    slots = ((first_rows // quarter) ^ own_quarter) * (quarter // span) + first_rows % quarter // span
    late = 3
    early = chips - late
    parts = []
    for w in range(2):
        parts.append(project(slots, pieces[w], out_held[:early], late))

    out_columns = w_out.shape[1] // 2
    weight_own = lax.dynamic_slice_in_dim(value_weight, core * out_columns, out_columns, 0)
    own_columns = [
        lax.dynamic_slice_in_dim(states, own_quarter * out_columns, out_columns, 1)
        for states in (hidden_in, states_got)
    ]
    pair_sums = jnp.stack(
        [
            finish(heads, out_held[early:], part, states, weight_own[None, :])[:2]
            for (part, heads), states in zip(parts, own_columns)
        ],
        1,
    )

    incoming, coming_old = suffix(known, place)
    advantage = local_part + bridge * coming_old + reach * incoming
    shared = swap(jnp.stack([advantage, old_values]))
    both_advantage = jnp.stack([advantage, shared[0]])
    both_old = jnp.stack([old_values, shared[1]])

    met = lax.ppermute(pair_sums, "mp", across)
    pair_sums = pair_sums + met
    turned = swap(pair_sums)
    pair_sums = pair_sums.reshape(2, 2, rows) + turned.reshape(2, 2, rows)[:, ::-1]
    value = pair_sums[1] * lax.rsqrt(pair_sums[0] / width + epsilon)
    returns = both_advantage + both_old
    clipped = both_old + jnp.clip(value - both_old, -clip_range, clip_range)
    terms = jnp.maximum((value - returns) ** 2, (clipped - returns) ** 2)
    window_loss = jnp.sum(terms, 1)
    total_loss = window_loss[:1] + window_loss[1:]
    by = 2
    while by < devices:
        total_loss = total_loss + lax.ppermute(
            total_loss, "dp", [(i, i ^ by) for i in range(devices)]
        )
        by *= 2
    value_loss = 0.5 * total_loss[0] / (rows * devices)
    return (value[0], advantage, value_loss)


def suits(devices, sides, hidden, query, key):
    return (
        sides == 2
        and devices >= 16
        and devices & (devices - 1) == 0
        and key[1] == 4 * HEAD
        and query[1] * devices == 8 * hidden[1]
        and hidden[0] % 512 == 0
    )


def body(hidden_in, w_query, w_key, *rest):
    fits = suits(
        lax.axis_size("dp"), lax.axis_size("mp"), hidden_in.shape, w_query.shape, w_key.shape
    )
    return (shared_body if fits else plain_body)(hidden_in, w_query, w_key, *rest)


def solution(mesh):
    return jax.shard_map(
        body,
        mesh=mesh,
        in_specs=(
            P("dp", None),
            P("dp", "mp"),
            P("dp", "mp"),
            P("dp", "mp"),
            P("dp", "mp"),
            P("mp"),
            P("dp"),
            P("dp"),
            P(),
            P(),
        ),
        out_specs=(P("dp"), P("dp"), P()),
        check_vma=False,
    )
```

```python
import math

import jax
import jax.numpy as jnp
from jax import lax
from jax.experimental import pallas as pl
from jax.experimental.pallas import tpu as pltpu
from jax.sharding import PartitionSpec as P


HEAD = 128


discount = 0.999
trace_decay = 0.997
clip_range = 0.2
epsilon = 1e-05
rope_base = 500000.0


def from_behind(array, axis, by):
    size = lax.axis_size(axis)
    pairs = [(i, i + by) for i in range(size) if 0 <= i + by < size]
    return lax.ppermute(array, axis, pairs)


def carried_in(part, axis, combine, identity):
    count = lax.axis_size(axis)
    place = lax.axis_index(axis)
    ahead = count - 1 - place
    gathered = jax.tree.map(lambda a: lax.all_gather(a, axis), part)
    state = jax.tree.map(lambda a, e: jnp.zeros_like(a) + jnp.asarray(e, a.dtype), part, identity)

    def one(hop, state):
        source = count - 1 - hop
        return combine(
            state, jax.tree.map(lambda a: lax.dynamic_index_in_dim(a, source, 0, False), gathered)
        )

    return lax.fori_loop(0, ahead, one, state)


def rotate(states, positions):
    half = HEAD // 2
    freq = rope_base ** (-jnp.arange(half, dtype=jnp.float32) * 2.0 / HEAD)
    angles = positions[:, None] * freq[None, :]
    cosine = jnp.cos(angles)[:, None, :]
    sine = jnp.sin(angles)[:, None, :]
    first = states[..., :half]
    second = states[..., half:]
    return jnp.concatenate([first * cosine - second * sine, second * cosine + first * sine], -1)


def plain_body(
    hidden_in, w_query, w_key, w_value, w_out, value_weight, rewards, old_values, lengths, terminal
):
    rows = hidden_in.shape[0]
    width = hidden_in.shape[1]
    states = hidden_in.astype(jnp.float32)
    normed = (states * lax.rsqrt(jnp.mean(states * states, 1, keepdims=True) + epsilon)).astype(
        jnp.bfloat16
    )
    pieces = (
        lax.all_gather(w_query, "dp", axis=0, tiled=True),
        lax.all_gather(w_key, "dp", axis=0, tiled=True),
        lax.all_gather(w_value, "dp", axis=0, tiled=True),
        lax.all_gather(w_out, "dp", axis=0, tiled=True),
    )
    add_pieces = pieces[:3]
    summed = tuple(
        (jnp.dot(normed, piece, preferred_element_type=jnp.float32) for piece in add_pieces)
    )
    stored = pieces[3]
    query_sum, key_sum, value_sum, whole_out = summed + (stored,)
    position_ids = lax.axis_index("dp") * rows + jnp.arange(rows, dtype=jnp.int32)
    positions = position_ids.astype(jnp.float32)
    local_heads = w_query.shape[1] // HEAD
    local_kv = w_key.shape[1] // HEAD
    group = local_heads // local_kv
    query = rotate(query_sum.reshape(rows, local_heads, HEAD), positions).astype(jnp.bfloat16)
    key = rotate(key_sum.reshape(rows, local_kv, HEAD), positions).astype(jnp.bfloat16)
    values_proj = value_sum.astype(jnp.bfloat16).reshape(rows, local_kv, HEAD)
    ends = jnp.cumsum(lengths)
    matches = ends[None, :] - 1 == position_ids[:, None]
    finished = jnp.any(matches, 1).astype(jnp.float32)
    stopped = jnp.sum(jnp.where(matches, terminal[None, :], 0), 1).astype(jnp.float32)
    episode = jnp.sum((ends[None, :] <= position_ids[:, None]).astype(jnp.int32), 1)
    order = jnp.arange(rows, dtype=jnp.int32)
    same_episode = episode[None, :] == episode[:, None]
    allowed = (order[None, :] <= order[:, None]) & same_episode
    scores = jnp.einsum(
        "tkgd,skd->kgts",
        query.reshape(rows, local_kv, group, HEAD),
        key,
        preferred_element_type=jnp.float32,
    ) * (1.0 / HEAD**0.5)
    masked = jnp.where(allowed[None, None], scores, -1e30)
    largest = jnp.max(masked, -1, keepdims=True)
    expon = jnp.where(allowed[None, None], jnp.exp(masked - largest), 0.0)
    probs = (expon / jnp.sum(expon, -1, keepdims=True)).astype(jnp.bfloat16)
    output = jnp.einsum("kgts,skd->tkgd", probs, values_proj, preferred_element_type=jnp.float32)
    attended = output.astype(jnp.bfloat16).reshape(rows, local_heads * HEAD)
    all_heads = lax.all_gather(attended, "mp", axis=1, tiled=True)
    projected = jnp.dot(all_heads, whole_out, preferred_element_type=jnp.float32)
    feature_count = w_out.shape[1]
    own_states = lax.dynamic_slice_in_dim(
        states, lax.axis_index("mp") * feature_count, feature_count, 1
    )
    residual = own_states + projected
    square_sum, head_sum = lax.psum(
        (jnp.sum(residual * residual, 1), jnp.sum(residual * value_weight[None, :], 1)), "mp"
    )
    value = head_sum * lax.rsqrt(square_sum / width + epsilon)
    following = from_behind(old_values[:1], "dp", -1)
    next_old = jnp.concatenate([old_values[1:], following])
    booted = jnp.where(finished > 0, (1.0 - stopped) * old_values, next_old)
    delta = rewards + discount * booted - old_values
    keep_rate = discount * trace_decay
    spacing = (order[None, :] - order[:, None]).astype(jnp.float32)
    forward_mask = (spacing >= 0.0) & same_episode
    decay_matrix = jnp.where(
        forward_mask, jnp.power(jnp.float32(keep_rate), jnp.maximum(spacing, 0.0)), 0.0
    )
    local_part = jnp.dot(decay_matrix, delta, precision=lax.Precision.HIGHEST)
    remaining = (rows - order).astype(jnp.float32)
    reach = jnp.where(episode == episode[-1], jnp.power(jnp.float32(keep_rate), remaining), 0.0) * (
        1.0 - finished[-1]
    )

    def compose(earlier, later_map):
        return (later_map[0] + later_map[1] * earlier[0], later_map[1] * earlier[1])

    prefix = carried_in(
        (local_part[:1], reach[:1]),
        "dp",
        compose,
        (jnp.zeros((1,), jnp.float32), jnp.ones((1,), jnp.float32)),
    )
    incoming = prefix[0][0]
    advantage = local_part + reach * incoming
    returns = advantage + old_values
    clipped = old_values + jnp.clip(value - old_values, -clip_range, clip_range)
    terms = jnp.maximum((value - returns) ** 2, (clipped - returns) ** 2)
    total_loss = lax.psum(jnp.sum(terms), "dp")
    value_loss = 0.5 * total_loss / (rows * lax.axis_size("dp"))
    return (value, advantage, value_loss)


def ring_order(chips):
    return list(range(0, chips, 2)) + list(range(chips - 1, 0, -2))


def ring_pairs(chips):
    order = ring_order(chips)
    pairs = []
    for spot in range(chips):
        here, there = order[spot], order[(spot + 1) % chips]
        pairs.append((2 * here, 2 * there))
        pairs.append((2 * there + 1, 2 * here + 1))
    return pairs


def ring_sources(chips):
    order = ring_order(chips)
    spots = {chip: spot for spot, chip in enumerate(order)}
    forward = [[order[(spots[c] - k) % chips] for k in range(chips)] for c in range(chips)]
    back = [[order[(spots[c] + k) % chips] for k in range(chips)] for c in range(chips)]
    return jnp.array([forward, back], jnp.int32)


def norm_kernel(sources, states_ref, normed_ref):
    width = states_ref.shape[1]
    chips = sources.shape[0]
    span = width // chips
    states = states_ref[...].astype(jnp.float32)
    scale = lax.rsqrt(jnp.mean(states * states, 1, keepdims=True) + epsilon)
    for k in range(chips):
        start = pl.multiple_of(sources[k] * span, span)
        piece = states_ref[:, pl.ds(start, span)].astype(jnp.float32)
        normed_ref[:, k * span : (k + 1) * span] = (piece * scale).astype(jnp.bfloat16)


def norm_in_order(states, sources, window, into=None):
    rows, width = states.shape
    tile = min(128, rows)
    steps = rows // tile
    operands = [states]
    specs = [pl.BlockSpec((tile, width), lambda i, s: (i, 0))]
    kernel = norm_kernel
    if into is not None:
        operands.append(into)
        specs.append(pl.BlockSpec(memory_space=pl.ANY))
        kernel = lambda s, x, _, o: norm_kernel(s, x, o)
    return pl.pallas_call(
        kernel,
        grid_spec=pltpu.PrefetchScalarGridSpec(
            num_scalar_prefetch=1,
            grid=(steps,),
            in_specs=specs,
            out_specs=pl.BlockSpec((tile, width), lambda i, s: (window * steps + i, 0)),
        ),
        out_shape=jax.ShapeDtypeStruct((2 * rows, width), jnp.bfloat16),
        input_output_aliases={} if into is None else {2: 0},
        cost_estimate=pl.CostEstimate(
            flops=4 * rows * width, bytes_accessed=4 * rows * width, transcendentals=rows
        ),
        compiler_params=pltpu.CompilerParams(vmem_limit_bytes=12 * 2**20),
    )(sources, *operands)


def spin(states, cosine, sine):
    return states * cosine + pltpu.roll(states, HEAD // 2, 1) * sine


def attend_kernel(window, query_ref, key_ref, val_ref, cos_ref, sin_ref, ep_col_ref, ep_row_ref, out_ref):
    rows = key_ref.shape[0]
    tile = rows // 2
    lane = lax.broadcasted_iota(jnp.int32, cos_ref.shape, 1)
    lower = lane < HEAD // 2

    def widen(table):
        turned = pltpu.roll(table, HEAD // 2, 1)
        return jnp.where(lower, table, turned) if window == 0 else jnp.where(lower, turned, table)

    cosine = widen(cos_ref[...])
    sine = widen(sin_ref[...])
    sine = jnp.where(lower, -sine, sine)
    key = spin(key_ref[...], cosine, sine).astype(jnp.bfloat16)
    vals = val_ref[...].astype(jnp.bfloat16)
    for t in range(2):
        low, high = t * tile, (t + 1) * tile
        at_row = lax.broadcasted_iota(jnp.int32, (tile, high), 0) + low
        at_col = lax.broadcasted_iota(jnp.int32, (tile, high), 1)
        allowed = (at_col <= at_row) & (ep_col_ref[low:high] == ep_row_ref[:, :high])
        bias = jnp.where(allowed, 0.0, -1e30)

        def some(step, _):
            for h in range(2):
                cut = pl.ds(pl.multiple_of((2 * step + h) * HEAD, HEAD), HEAD)
                query = spin(query_ref[low:high, cut], cosine[low:high], sine[low:high])
                scores = lax.dot_general(
                    query.astype(jnp.bfloat16),
                    key[:high],
                    (((1,), (1,)), ((), ())),
                    preferred_element_type=jnp.float32,
                )
                masked = scores * (1.0 / HEAD**0.5) + bias
                largest = jnp.max(masked, -1, keepdims=True)
                expon = jnp.exp(masked - largest)
                share = 1.0 / jnp.sum(expon, -1, keepdims=True)
                probs = (expon * share).astype(jnp.bfloat16)
                out_ref[low:high, cut] = jnp.dot(
                    probs, vals[:high], preferred_element_type=jnp.float32
                ).astype(jnp.bfloat16)
            return 0

        lax.fori_loop(0, query_ref.shape[1] // HEAD // 2, some, 0)


def attend(window, which, rows, query, kv, cosine, sine, ep_col, ep_row):
    kv_count = kv.shape[1] // HEAD // 2
    width = query.shape[1]
    heads = width // HEAD
    once = lambda i: (window, 0)
    return pl.pallas_call(
        lambda *refs: attend_kernel(window, *refs),
        grid=(1,),
        in_specs=[
            pl.BlockSpec((rows, width), once),
            pl.BlockSpec((rows, HEAD), lambda i: (window, which)),
            pl.BlockSpec((rows, HEAD), lambda i: (window, kv_count + which)),
            pl.BlockSpec((rows, HEAD), lambda i: (0, 0)),
            pl.BlockSpec((rows, HEAD), lambda i: (0, 0)),
            pl.BlockSpec((rows, 1), once),
            pl.BlockSpec((1, rows), lambda i: (0, window)),
        ],
        out_specs=pl.BlockSpec((rows, width), lambda i: (0, 0)),
        out_shape=jax.ShapeDtypeStruct((rows, width), jnp.bfloat16),
        cost_estimate=pl.CostEstimate(
            flops=4 * heads * HEAD * rows * rows,
            bytes_accessed=6 * rows * width,
            transcendentals=heads * rows * rows,
        ),
        compiler_params=pltpu.CompilerParams(vmem_limit_bytes=12 * 2**20),
    )(query, kv, kv, cosine, sine, ep_col, ep_row)


def project_kernel(pieces, count, late, *refs):
    offsets = refs[0]
    piece_refs = refs[1 : 1 + pieces]
    weight_refs = refs[1 + pieces : 1 + pieces + 2 * count]
    total_ref, late_ref, heads_ref, weights, sems = refs[1 + pieces + 2 * count :]
    rows = piece_refs[0].shape[0]
    half = weights.shape[2]
    copies = [(ref, heads_ref.at[p]) for p, ref in enumerate(piece_refs)]
    copies += [(ref, weights.at[i]) for i, ref in enumerate(weight_refs)]
    copies = [pltpu.make_async_copy(*c, sems.at[i]) for i, c in enumerate(copies)]
    for copy in copies:
        copy.start()
    for copy in copies[:pieces]:
        copy.wait()
    for k in range(late):
        late_ref[k] = heads_ref[offsets[count + k]]
    tile = 256
    for k in range(count):
        copies[pieces + 2 * k].wait()
        copies[pieces + 2 * k + 1].wait()

    def one(step, _):
        at = pl.ds(pl.multiple_of(step * tile, tile), tile)
        for side in range(2):
            total = None
            for k in range(count):
                term = jnp.dot(
                    heads_ref[offsets[k], at],
                    weights[2 * k + side],
                    preferred_element_type=jnp.float32,
                )
                total = term if total is None else total + term
            total_ref[at, side * half : (side + 1) * half] = total
        return 0

    lax.fori_loop(0, rows // tile, one, 0)


def project(offsets, pieces, pairs, late):
    weights = [w for pair in pairs for w in pair]
    rows, span = pieces[0].shape
    half = weights[0].shape[1]
    number = len(pieces)
    count = len(pairs)
    here = pl.BlockSpec(memory_space=pltpu.HBM)
    vmem = pl.BlockSpec(memory_space=pltpu.VMEM)
    return pl.pallas_call(
        lambda *refs: project_kernel(number, count, late, *refs),
        in_specs=[pl.BlockSpec(memory_space=pltpu.SMEM)] + [here] * (number + len(weights)),
        out_specs=[vmem, vmem],
        out_shape=[
            jax.ShapeDtypeStruct((rows, 2 * half), jnp.float32),
            jax.ShapeDtypeStruct((late, rows, span), jnp.bfloat16),
        ],
        scratch_shapes=[
            pltpu.VMEM((number, rows, span), jnp.bfloat16),
            pltpu.VMEM((len(weights), span, half), jnp.bfloat16),
            pltpu.SemaphoreType.DMA((number + len(weights),)),
        ],
        compiler_params=pltpu.CompilerParams(vmem_limit_bytes=20 * 2**20),
        cost_estimate=pl.CostEstimate(
            flops=4 * rows * half * span * count,
            bytes_accessed=2 * rows * span * number + 8 * rows * half,
            transcendentals=0,
        ),
        name="project",
    )(offsets, *pieces, *weights)


def finish_kernel(late, *refs):
    heads_refs, refs = refs[:2], refs[2:]
    weights, refs = refs[: 2 * late], refs[2 * late :]
    base_refs, states_refs, (weight_ref, out_ref) = refs[:2], refs[2:4], refs[4:]
    half = weights[0].shape[1]
    for w in range(2):
        squares = headed = 0.0
        for side in range(2):
            cut = slice(side * half, (side + 1) * half)
            total = base_refs[w][:, cut]
            for k in range(late):
                total = total + jnp.dot(
                    heads_refs[w][k],
                    weights[2 * k + side][...],
                    preferred_element_type=jnp.float32,
                )
            residual = total + states_refs[w][:, cut].astype(jnp.float32)
            squares = squares + jnp.sum(residual * residual, 1, keepdims=True)
            headed = headed + jnp.sum(residual * weight_ref[:, cut], 1, keepdims=True)
        lane = lax.broadcasted_iota(jnp.int32, (squares.shape[0], HEAD), 1)
        out_ref[w] = jnp.where(lane == 0, squares, headed).T[: out_ref.shape[1]]


def finish(heads, pairs, bases, states, weight):
    late, rows, span = heads[0].shape
    columns = bases[0].shape[1]
    weights = [w for pair in pairs for w in pair]
    tile = 256
    whole = lambda i: (0, 0)
    return pl.pallas_call(
        lambda *refs: finish_kernel(late, *refs),
        grid=(rows // tile,),
        in_specs=[pl.BlockSpec((late, tile, span), lambda i: (0, i, 0))] * 2
        + [pl.BlockSpec(w.shape, whole) for w in weights]
        + [pl.BlockSpec((tile, columns), lambda i: (i, 0))] * 4
        + [pl.BlockSpec((1, columns), whole)],
        out_specs=pl.BlockSpec((2, 8, tile), lambda i: (0, 0, i)),
        out_shape=jax.ShapeDtypeStruct((2, 8, rows), jnp.float32),
        compiler_params=pltpu.CompilerParams(vmem_limit_bytes=20 * 2**20),
        cost_estimate=pl.CostEstimate(
            flops=4 * rows * columns * span * late,
            bytes_accessed=2 * rows * (2 * late * span + 6 * columns),
            transcendentals=0,
        ),
        name="finish",
    )(*heads, *weights, *bases, *states, weight)


def loss_kernel(width, sums_ref, turned_ref, advantage_ref, old_ref, value_ref, loss_ref):
    losses = []
    for w in range(2):
        squares = sums_ref[w, 0:1] + turned_ref[1 - w, 0:1]
        headed = sums_ref[w, 1:2] + turned_ref[1 - w, 1:2]
        value = headed * lax.rsqrt(squares / width + epsilon)
        old = old_ref[w : w + 1]
        returns = advantage_ref[w : w + 1] + old
        clipped = old + jnp.clip(value - old, -clip_range, clip_range)
        terms = jnp.maximum((value - returns) ** 2, (clipped - returns) ** 2)
        losses.append(jnp.sum(terms, 1, keepdims=True))
        if w == 0:
            value_ref[...] = value
    loss_ref[...] = jnp.broadcast_to(losses[0] + losses[1], loss_ref.shape)


def window_losses(sums, turned, advantage, old, width):
    vmem = pl.BlockSpec(memory_space=pltpu.VMEM)
    rows = old.shape[1]
    return pl.pallas_call(
        lambda *refs: loss_kernel(width, *refs),
        in_specs=[vmem] * 4,
        out_specs=[vmem] * 2,
        out_shape=[
            jax.ShapeDtypeStruct((1, rows), jnp.float32),
            jax.ShapeDtypeStruct((1, HEAD), jnp.float32),
        ],
        compiler_params=pltpu.CompilerParams(vmem_limit_bytes=2 * 2**20),
        name="losses",
    )(sums, turned, advantage, old)


def tie(array, *others):
    return lax.optimization_barrier((array,) + others)[0]


def suffix_kernel(place_ref, maps_ref, out_ref):
    devices = maps_ref.shape[0]
    place = place_ref[0]
    total, old = jnp.float32(0.0), jnp.float32(0.0)
    for i in range(devices - 1, 0, -1):
        later = i > place
        fresh = maps_ref[i, 0] + maps_ref[i, 1] * old + maps_ref[i, 2] * total
        total = jnp.where(later, fresh, total)
        old = jnp.where(later, maps_ref[i, 3], old)
    out_ref[0] = total
    out_ref[1] = old


def suffix(maps, place):
    smem = pl.BlockSpec(memory_space=pltpu.SMEM)
    out = pl.pallas_call(
        suffix_kernel,
        in_specs=[smem, smem],
        out_specs=smem,
        out_shape=jax.ShapeDtypeStruct((2,), jnp.float32),
        compiler_params=pltpu.CompilerParams(vmem_limit_bytes=2**20),
        name="suffix",
    )(place.astype(jnp.int32).reshape(1), maps)
    return out[0], out[1]


def tie(array, *others):
    return lax.optimization_barrier((array,) + others)[0]


def shared_body(
    hidden_in, w_query, w_key, w_value, w_out, value_weight, rewards, old_values, lengths, terminal
):
    rows, width = hidden_in.shape
    devices = lax.axis_size("dp")
    place = lax.axis_index("dp")
    side = lax.axis_index("mp")
    core = place % 2
    chip = place // 2
    chips = devices // 2
    partner = [(i, i ^ 1) for i in range(devices)]
    across = [(0, 1), (1, 0)]
    ring = ring_pairs(chips)

    def swap(array):
        return lax.ppermute(array, "dp", partner)

    def pair_up(mine, got):
        return jnp.where(
            core == 0, jnp.concatenate([mine, got], 0), jnp.concatenate([got, mine], 0)
        )

    def columns(weight, which, part, parts):
        half = weight.shape[1] // 2
        size = half // parts
        return lax.dynamic_slice_in_dim(weight, which * half + part * size, size, 1)

    def chip_block(pieces):
        mine = jnp.concatenate([columns(w, core, *p) for w, *p in pieces], 1)
        theirs = jnp.concatenate([columns(w, 1 - core, *p) for w, *p in pieces], 1)
        return pair_up(mine, swap(theirs))

    local_kv = w_key.shape[1] // HEAD // 2
    group = w_query.shape[1] // w_key.shape[1]

    def hop(block):
        return lax.ppermute(block, "dp", ring)

    lanes = [chip_block([(w_key, 0, 1), (w_value, 0, 1)])]
    lanes += [chip_block([(w_query, j, local_kv)]) for j in range(local_kv)]
    first_hops = [hop(block) for block in lanes]
    states_got = swap(hidden_in)
    sources = ring_sources(chips)[core, chip]
    span = width // chips

    def marks(place, lengths):
        ends = jnp.cumsum(lengths)
        order = jnp.arange(rows, dtype=jnp.int32)
        position_ids = place * rows + order
        other_ids = (place + 1 - 2 * core) * rows + order
        both_ids = jnp.concatenate([position_ids, other_ids])
        half = HEAD // 2
        lane = jnp.arange(HEAD, dtype=jnp.int32)
        freq = rope_base ** (-(lane % half).astype(jnp.float32) * 2.0 / HEAD)
        spot = jnp.where(lane[None, :] < half, position_ids[:, None], other_ids[:, None])
        angles = spot.astype(jnp.float32) * freq[None, :]
        cosine = jnp.cos(angles)
        sine = jnp.sin(angles)
        both_episode = jnp.sum((ends[None, :] <= both_ids[:, None]).astype(jnp.int32), 1)
        return cosine, sine, both_episode, ends, position_ids, order

    def steps(place, marked, terminal, rewards, old_values):
        both_episode, ends, position_ids, order = marked
        matches = ends[None, :] - 1 == position_ids[:, None]
        finished = jnp.any(matches, 1).astype(jnp.float32)
        stopped = jnp.sum(jnp.where(matches, terminal[None, :], 0), 1).astype(jnp.float32)
        episode = both_episode[:rows]
        same_episode = episode[None, :] == episode[:, None]
        next_known = jnp.concatenate([old_values[1:], jnp.zeros((1,), jnp.float32)])
        booted = jnp.where(finished > 0, (1.0 - stopped) * old_values, next_known)
        delta = rewards + discount * booted - old_values
        keep_rate = discount * trace_decay

        def powers(number):
            return jnp.exp(number * math.log(keep_rate))

        spacing = (order[None, :] - order[:, None]).astype(jnp.float32)
        forward_mask = (spacing >= 0.0) & same_episode
        decay_matrix = jnp.where(
            forward_mask, powers(jnp.maximum(spacing, 0.0)), 0.0
        )
        local_part = jnp.dot(decay_matrix, delta, precision=lax.Precision.HIGHEST)
        remaining = (rows - order).astype(jnp.float32)
        open_end = 1.0 - finished[-1]
        reach = jnp.where(episode == episode[-1], powers(remaining), 0.0) * open_end
        bridge = reach / trace_decay
        row = lax.broadcasted_iota(jnp.int32, (devices, 4), 0)
        column = lax.broadcasted_iota(jnp.int32, (devices, 4), 1)
        known = jnp.where(column == 0, local_part[0], old_values[0])
        known = jnp.where(column == 1, bridge[0], jnp.where(column == 2, reach[0], known))
        known = jnp.where(row == place, known, 0.0)
        return local_part, bridge, reach, known

    normed = norm_in_order(hidden_in, sources, 0)
    normed = norm_in_order(states_got, sources, 1, normed)

    def use(total, k, block):
        term = jnp.dot(
            normed[:, k * span : (k + 1) * span], block, preferred_element_type=jnp.float32
        )
        return term if total is None else total + term

    sums = [use(None, 0, block) for block in lanes]
    blocks = first_hops
    for k in range(1, chips):
        if k + 1 < chips:
            coming = [hop(block) for block in blocks]
        sums = [use(sums[lane], k, block) for lane, block in enumerate(blocks)]
        if k == 4:
            *later, _ = lax.optimization_barrier((place, lengths, sums[0]))
            cosine, sine, *marked = marks(*later)
            both_episode = marked[0]
        if k == 5:
            *later, _ = lax.optimization_barrier(
                (place, tuple(marked), terminal, rewards, old_values, sums[0])
            )
            local_part, bridge, reach, known = steps(*later)
        step = 2 ** max(k - 6, 0)
        if k > 5:
            moved = lax.ppermute(
                tie(known, blocks[0]), "dp", [(i, i ^ step) for i in range(devices)]
            )
            known = known + moved
        if k == chips - 3:
            out_blocks = [chip_block([(tie(w_out, blocks[0]), j, 2)]) for j in range(2)]
        if 3 <= k < chips - 1:
            sums = [tie(total, blocks[0]) for total in sums]
        last_blocks = blocks
        blocks = coming
    out_held = [out_blocks]
    for k in range(1, chips):
        out_held.append(
            [
                hop(tie(block, last_blocks[j]) if k == 1 else block)
                for j, block in enumerate(out_held[-1])
            ]
        )

    number = chips - 6
    while 2**number < devices:
        step = 2**number
        moved = lax.ppermute(
            tie(known, out_held[2 * number - 2][0]), "dp", [(i, i ^ step) for i in range(devices)]
        )
        known = known + moved
        number += 1
    pieces = [[], []]
    sent = {}
    for w in range(2):
        for j in range(local_kv):
            part = attend(
                w, j, rows, sums[1 + j], sums[0], cosine, sine,
                both_episode[:, None], both_episode[None, :],
            )
            sent[w, j] = (part, lax.ppermute(part, "mp", across))
    diagonal = {}
    for n, (w, j) in enumerate((w, j) for w in range(2) for j in range(local_kv)):
        after = out_held[min(n + 2, chips - 2)]
        diagonal[1 - w, j] = swap(tie(sent[w, j][1], *after))
    for w in range(2):
        pieces[w] = [sent[w, j][0] for j in range(local_kv)]
        pieces[w] += [swap(sent[1 - w, j][0]) for j in range(local_kv)]
        pieces[w] += [sent[w, j][1] for j in range(local_kv)]
        pieces[w] += [diagonal[w, j] for j in range(local_kv)]

    quarter = local_kv * group * HEAD
    own_quarter = side * 2 + core
    first_rows = sources * span
    slots = ((first_rows // quarter) ^ own_quarter) * (quarter // span) + first_rows % quarter // span
    late = 2
    early = chips - late
    parts = []
    for w in range(2):
        parts.append(project(slots, pieces[w], out_held[:early], late))

    out_columns = w_out.shape[1] // 2
    weight_own = lax.dynamic_slice_in_dim(value_weight, core * out_columns, out_columns, 0)
    own_columns = [
        lax.dynamic_slice_in_dim(states, own_quarter * out_columns, out_columns, 1)
        for states in (hidden_in, states_got)
    ]
    pair_sums = finish(
        [heads for _, heads in parts],
        out_held[early:],
        [part for part, _ in parts],
        own_columns,
        weight_own[None, :],
    )

    incoming, coming_old = suffix(known, place)
    advantage = local_part + bridge * coming_old + reach * incoming
    shared = swap(jnp.stack([advantage, old_values]))
    both_advantage = jnp.stack([advantage, shared[0]])
    both_old = jnp.stack([old_values, shared[1]])

    met = lax.ppermute(pair_sums, "mp", across)
    pair_sums = pair_sums + met
    turned = swap(pair_sums)
    value, total_loss = window_losses(pair_sums, turned, both_advantage, both_old, width)
    by = 2
    while by < devices:
        total_loss = total_loss + lax.ppermute(
            total_loss, "dp", [(i, i ^ by) for i in range(devices)]
        )
        by *= 2
    value_loss = 0.5 * total_loss[0, 0] / (rows * devices)
    return (value.reshape(rows), advantage, value_loss)


def suits(devices, sides, hidden, query, key):
    return (
        sides == 2
        and devices >= 16
        and devices & (devices - 1) == 0
        and key[1] == 4 * HEAD
        and query[1] * devices == 8 * hidden[1]
        and hidden[0] % 512 == 0
    )


def body(hidden_in, w_query, w_key, *rest):
    fits = suits(
        lax.axis_size("dp"), lax.axis_size("mp"), hidden_in.shape, w_query.shape, w_key.shape
    )
    return (shared_body if fits else plain_body)(hidden_in, w_query, w_key, *rest)


def solution(mesh):
    return jax.shard_map(
        body,
        mesh=mesh,
        in_specs=(
            P("dp", None),
            P("dp", "mp"),
            P("dp", "mp"),
            P("dp", "mp"),
            P("dp", "mp"),
            P("mp"),
            P("dp"),
            P("dp"),
            P(),
            P(),
        ),
        out_specs=(P("dp"), P("dp"), P()),
        check_vma=False,
    )
```
